512 devices in a mesh: lat: 16 (over y, core), lon: 32 (over z, x).
Axes of the slice: x: 4, y: 8, z: 8, core: 2. Of those that a mesh axis runs over, the one named last changes fastest.
Arguments:
- adjoint_in: float32 [4, 72, 128, 4096], P(None, None, 'lat', 'lon'), may hold values from -6 to 6
- wind_u: float32 [72, 128, 4096], P(None, 'lat', 'lon'), may hold values from -0.45 to 0.45
- wind_v: float32 [72, 128, 4096], P(None, 'lat', 'lon'), may hold values from -0.45 to 0.45
- diffusion: float32 [72, 128, 4096], P(None, 'lat', 'lon'), may hold values from 0.02 to 8
- kernel_rows: bfloat16 [72, 1048576], P(None, ('lat', 'lon')), may hold values from 0 to 1
- retrieval_misfit: bfloat16 [4, 1048576], P(None, ('lat', 'lon')), may hold values from -6 to 6
- retrieval_columns: int32 [1048576], P(('lat', 'lon')), may hold values from 0 to 32767, as said below
- retrieval_counts: int32 [512], P(('lat', 'lon')), may hold values from 128 to 2048, as said below
- station_cells: int32 [8192], P(('lat', 'lon')), may hold values from 0 to 1023
- station_misfit: float32 [4, 8192], P(None, ('lat', 'lon')), may hold values from -6 to 6
Outputs:
- adjoint_out: float32 [4, 72, 128, 4096], P(None, None, 'lat', 'lon')
The draws below stay inside these ranges and needn't reach their ends.
Inputs may be any that keep to these rules, and one draw needn't show every extreme that they name: Only the first retrieval_counts slots of a device hold live retrievals; in each latitude band one device holds 2048. `retrieval_columns`: each value names a tile of the holding device's latitude band (value // 1024) and a cell of it (row times 128 plus column). Among the live retrievals of one device at most 128 name one tile, and in each band one tile is named by exactly 128 live retrievals of every device of the band.
All inputs are finite; a program needn't handle non-finite values.
Results may differ from the reference program's by a relative error of at most 0.0003.
Values may be sent and summed in bfloat16 or wider, within the bound.
No kernel may reach another device: no remote copies, remote signals or barrier semaphores. Data moves between devices by JAX's collectives and lax.ppermute only.
A program may use at most 128 MiB of HBM per device.

```python
import math
import jax
import jax.numpy as jnp

NTR = 4
L = 72
CLAT = 8
CLON = 128
R_DEV = 2048
S_DEV = 16
COLS = 1024
CAP = 128
NLAT = 128
NLON = 4096
RETR = 1048576
STATIONS = 8192
N_LAT = 16
N_LON = 32


def band_layout(key):
    hot_key, count_key, order_key, cell_key = jax.random.split(key, 4)
    devices = N_LAT * N_LON
    hottest = jax.random.randint(hot_key, (N_LAT,), 0, N_LON)
    spread = jax.random.randint(count_key, (N_LAT, N_LON), 8, 33)
    busiest = (hottest + 1) % N_LON
    spread = jnp.where(jnp.arange(N_LON)[None, :] == busiest[:, None], 32, spread)
    counts = (CAP + (R_DEV - CAP) * spread * spread // 1024).reshape(devices)
    hot_tiles = jnp.repeat(hottest, N_LON)
    position = jnp.arange(R_DEV)

    def one_device(device_key, hot_tile, count):
        first_key, second_key, third_key = jax.random.split(device_key, 3)
        others = jax.random.permutation(first_key, N_LON - 1)
        cyclic = others[jnp.maximum(position - CAP, 0) % (N_LON - 1)]
        base = jnp.where(position < CAP, hot_tile, (hot_tile + 1 + cyclic) % N_LON)
        noise = jax.random.randint(second_key, (R_DEV,), 0, 4096)
        score = jnp.where(position < CAP, position, R_DEV + noise * R_DEV + position)
        mixed = base[jnp.argsort(score, stable=True)]
        noise_two = jax.random.randint(third_key, (R_DEV,), 0, 4096)
        score_two = jnp.where(position < count, noise_two * R_DEV + position, 4096 * R_DEV + position)
        return mixed[jnp.argsort(score_two, stable=True)]
    device_keys = jax.random.split(order_key, devices)
    tiles = jax.vmap(one_device)(device_keys, hot_tiles, counts)
    cells = jax.random.randint(cell_key, (devices, R_DEV), 0, CLAT * CLON)
    columns = (tiles * (CLAT * CLON) + cells).reshape(devices * R_DEV).astype(jnp.int32)
    return (columns, counts.astype(jnp.int32))


def draw_retrieval_columns(key, part):
    return band_layout(jax.random.fold_in(key, 11))[0]


def draw_retrieval_counts(key, part):
    return band_layout(jax.random.fold_in(key, 11))[1]


def touch_ends(values, rng, least, high):
    longest = values.shape.index(max(values.shape))
    spots = []
    for shift in (0, 1):
        where = [jax.random.randint(jax.random.fold_in(rng, axis), (), 0, length) for axis, length in enumerate(values.shape)]
        where[longest] = (where[longest] + shift) % values.shape[longest]
        spots.append(tuple(where))
    return values.at[spots[0]].set(least).at[spots[1]].set(high)


def level_of(rng, dims, cuts, least, high):
    loudness, own = 1.0, jax.random.fold_in(rng, 6)
    for dim, shards_of in cuts:
        heights = jnp.exp(jax.random.uniform(jax.random.fold_in(own, dim), (shards_of,), jnp.float32, least / len(cuts), high / len(cuts)))
        loudness = loudness * jnp.repeat(heights, dims[dim] // shards_of).reshape([-1 if axis == dim else 1 for axis in range(len(dims))])
    return loudness


def gaussian(own_key, dims, scale, bound, shards=(), kind=jnp.bfloat16):
    values = jax.random.normal(own_key, dims, jnp.float32) * scale
    if len(shards) > 0:
        values = level_of(own_key, dims, shards, -0.22, 0.18) * values
    return jnp.clip(values, min=-bound, max=bound).astype(kind)


def setup_inputs(seed: int = 0) -> dict:
    key_list = jax.random.split(jax.random.key(seed), 11)
    return {
        "adjoint_in": gaussian(key_list[0], (NTR, L, NLAT, NLON), 1.0, 6.0, ((2, 16), (3, 32)), jnp.float32),
        "wind_u": jnp.clip(jax.random.uniform(key_list[1], (L, NLAT, NLON), jnp.float32, -0.45, 0.45) * level_of(key_list[1], (L, NLAT, NLON), ((1, 16), (2, 32)), -0.4, 0.0), -0.45, 0.45),
        "wind_v": jnp.clip(jax.random.uniform(key_list[2], (L, NLAT, NLON), jnp.float32, -0.45, 0.45) * level_of(key_list[2], (L, NLAT, NLON), ((1, 16), (2, 32)), -0.4, 0.0), -0.45, 0.45),
        "diffusion": jnp.clip(jnp.exp(math.log(8.0) - 5.9914646 * jax.random.uniform(key_list[3], (L, NLAT, NLON), jnp.float32) ** level_of(key_list[3], (L, NLAT, NLON), ((1, 16), (2, 32)), -0.2, 0.2)), 0.02, 8.0),
        "kernel_rows": jnp.clip(1.0 * jax.random.uniform(key_list[4], (L, RETR), jnp.float32) ** level_of(key_list[4], (L, RETR), ((1, 512),), -0.2, 0.2), 0.0, 1.0).astype(jnp.bfloat16),
        "retrieval_misfit": gaussian(key_list[5], (NTR, RETR), 1.0, 6.0, ((1, 512),)),
        "retrieval_columns": draw_retrieval_columns(jax.random.fold_in(key_list[10], 71), 0),
        "retrieval_counts": draw_retrieval_counts(jax.random.fold_in(key_list[10], 71), 0),
        "station_cells": touch_ends(jax.random.randint(key_list[8], (STATIONS,), 0, COLS), jax.random.fold_in(key_list[8], 1), 0, COLS - 1).astype(jnp.int32),
        "station_misfit": gaussian(key_list[9], (NTR, STATIONS), 1.0, 6.0, ((1, 512),), jnp.float32),
    }


def pad_global(field):
    wide = jnp.pad(field, ((0, 0), (0, 0), (1, 1), (0, 0)))
    return jnp.concatenate([wide[..., -1:], wide, wide[..., :1]], axis=3)


def advect(padded, wind_u, wind_v):
    centre = padded[:, :, 1:-1, 1:-1]
    east = padded[:, :, 1:-1, 2:]
    west = padded[:, :, 1:-1, :-2]
    north = padded[:, :, 2:, 1:-1]
    south = padded[:, :, :-2, 1:-1]
    result = centre + jnp.maximum(wind_u, 0.0) * (east - centre)
    result = result + jnp.maximum(-wind_u, 0.0) * (west - centre)
    result = result + jnp.maximum(wind_v, 0.0) * (north - centre)
    result = result + jnp.maximum(-wind_v, 0.0) * (south - centre)
    return result


def factor(diffusion):
    levels = diffusion.shape[0]
    inverse = [1.0 / (1.0 + diffusion[0])]
    for level in range(1, levels):
        below = diffusion[level - 1]
        weight = 1.0 + below + diffusion[level] - below * below * inverse[level - 1]
        inverse.append(1.0 / weight)
    upper = [diffusion[level] * inverse[level] for level in range(levels - 1)]
    return inverse, upper


def relax(field, diffusion, inverse, upper):
    levels = diffusion.shape[0]
    sweep = [field[:, 0] * inverse[0]]
    for level in range(1, levels):
        sweep.append((field[:, level] + diffusion[level - 1] * sweep[-1]) * inverse[level])
    result = [sweep[-1]]
    for level in range(levels - 2, -1, -1):
        result.append(sweep[level] + upper[level] * result[-1])
    ordered = result[::-1]
    return jnp.stack(ordered, axis=1)


def advance(field, wind_u, wind_v, diffusion, inverse, upper):
    return relax(advect(pad_global(field), wind_u, wind_v), diffusion, inverse, upper)


def reference(adjoint_in, wind_u, wind_v, diffusion, kernel_rows, retrieval_misfit, retrieval_columns, retrieval_counts, station_cells, station_misfit):
    cells_total = NLAT * NLON
    holder = jnp.arange(STATIONS, dtype=jnp.int32) // S_DEV
    band = holder // N_LON
    tile = holder % N_LON
    row = band * CLAT + station_cells // CLON
    column = tile * CLON + station_cells % CLON
    place = (row * NLON + column).astype(jnp.int32)
    surface = jax.ops.segment_sum(station_misfit.T, place, num_segments=cells_total)
    started = adjoint_in.at[:, 0].add(surface.T.reshape(NTR, NLAT, NLON))
    inverse, upper = factor(diffusion)
    first = advance(started, wind_u, wind_v, diffusion, inverse, upper)
    slot = jnp.arange(RETR, dtype=jnp.int32)
    owner = slot // R_DEV
    live = (slot % R_DEV) < retrieval_counts[owner]
    rband = owner // N_LON
    rtile = retrieval_columns // COLS
    rcell = retrieval_columns % COLS
    rrow = rband * CLAT + rcell // CLON
    rcolumn = rtile * CLON + rcell % CLON
    rplace = (rrow * NLON + rcolumn).astype(jnp.int32)
    rows_wide = kernel_rows.astype(jnp.float32).T
    pieces = []
    for tracer in range(NTR):
        weight = jnp.where(live, retrieval_misfit[tracer].astype(jnp.float32), jnp.float32(0.0))
        summed = jax.ops.segment_sum(rows_wide * weight[:, None], rplace, num_segments=cells_total)
        pieces.append(summed.T.reshape(L, NLAT, NLON))
    injected = first + jnp.stack(pieces, axis=0)
    field = advance(injected, wind_u, wind_v, diffusion, inverse, upper)
    return advance(field, wind_u, wind_v, diffusion, inverse, upper)
```

```python
import functools

import jax
import jax.numpy as jnp
from jax import lax
from jax.experimental import pallas as pl
from jax.experimental.pallas import tpu as pltpu
from jax.sharding import PartitionSpec as P

F32 = jnp.float32
BF16 = jnp.bfloat16
PARAMS = pltpu.CompilerParams(vmem_limit_bytes=56 << 20)
GROUP = 8


def lanes_iota():
    return lax.broadcasted_iota(jnp.int32, (8, 128), 1)


def rows_iota():
    return lax.broadcasted_iota(jnp.int32, (8, 128), 0)


def pack_kernel(count_ref, rows_ref, misfit_ref, columns_ref, out_ref):
    chunks = columns_ref.shape[0]
    tiles = out_ref.shape[0]
    count = count_ref[0]
    lane = lax.broadcasted_iota(jnp.int32, (1, 128), 1)
    tile = lax.broadcasted_iota(jnp.int32, (tiles, 128), 0)
    hits = []
    targets = []
    misc = []
    for j in range(chunks):
        column = columns_ref[j : j + 1, :]
        live = (lane + j * 128) < count
        target = jnp.where(live, column >> 10, -1)
        targets.append(target)
        hits.append((tile == target).astype(F32))
        cell = column & 1023
        misc.append(
            jnp.concatenate(
                [
                    misfit_ref[:, j * 128 : (j + 1) * 128].astype(F32),
                    (cell >> 7).astype(F32),
                    (cell & 127).astype(F32),
                    jnp.zeros((2, 128), F32),
                ],
                axis=0,
            )
        )
    before = lax.broadcasted_iota(jnp.int32, (128, 128), 0) < lax.broadcasted_iota(
        jnp.int32, (128, 128), 1
    )
    prefix = jnp.dot(
        jnp.concatenate(hits, axis=0).astype(BF16),
        before.astype(F32).astype(BF16),
        preferred_element_type=F32,
    )
    offset = jnp.zeros((tiles, 1), F32)
    ranks = []
    for j in range(chunks):
        rank = jnp.sum(
            hits[j] * (prefix[j * tiles : (j + 1) * tiles] + offset), axis=0, keepdims=True
        )
        ranks.append(rank)
        offset = offset + jnp.sum(hits[j], axis=1, keepdims=True)
    tail = jnp.concatenate(
        [rows_ref[64:72, :].astype(F32), jnp.concatenate(misc, axis=1)], axis=0
    ).astype(BF16)
    payload = jnp.concatenate([rows_ref[0:64, :], tail], axis=0)
    target = jnp.concatenate(targets, axis=1)
    rank = jnp.concatenate(ranks, axis=1)
    slot = lax.broadcasted_iota(jnp.int32, (128, chunks * 128), 0).astype(F32).astype(BF16)
    one = jnp.ones((128, chunks * 128), BF16)
    zero = jnp.zeros((128, chunks * 128), BF16)
    for pair in range(tiles // 2):
        parts = []
        for side in range(2):
            key = jnp.where(target == 2 * pair + side, rank, -1.0).astype(BF16)
            parts.append(jnp.where(slot == key, one, zero))
        chosen = jnp.concatenate(parts, axis=0)
        packed = lax.dot_general(
            payload, chosen, (((1,), (1,)), ((), ())), preferred_element_type=F32
        ).astype(BF16)
        out_ref[2 * pair] = packed[:, :128]
        out_ref[2 * pair + 1] = packed[:, 128:]


def rows_out(field_ref, up_ref, down_ref):
    count = up_ref.shape[0]
    up_ref[...] = field_ref[pl.ds(7, count, stride=8), :]
    down_ref[...] = field_ref[pl.ds(0, count, stride=8), :]


def columns_out(field_ref, east_ref, west_ref, levels):
    tracers = east_ref.shape[0]
    lane = lanes_iota()

    def group(g, carry):
        east, west = list(carry[0]), list(carry[1])
        for j in range(GROUP):
            level = g * GROUP + j
            here = lane == level
            for t in range(tracers):
                x = field_ref[pl.ds((t * levels + level) * 8, 8), :]
                east[t] = jnp.where(here, pltpu.roll(x, level + 1, 1), east[t])
                west[t] = jnp.where(here, pltpu.roll(x, level, 1), west[t])
        return tuple(east), tuple(west)

    zero = tuple(jnp.zeros((8, 128), F32) for _ in range(tracers))
    east, west = lax.fori_loop(0, levels // GROUP, group, (zero, zero))
    for t in range(tracers):
        east_ref[t] = east[t]
        west_ref[t] = west[t]


def prep_kernel(
    cells_ref,
    weights_ref,
    field_ref,
    diffusion_ref,
    started_ref,
    inverse_ref,
    up_ref,
    down_ref,
    east_ref,
    west_ref,
):
    levels = diffusion_ref.shape[0] // 8
    tracers = field_ref.shape[0] // (8 * levels)
    cell = rows_iota() * 128 + lanes_iota()
    started_ref[...] = field_ref[...]
    for t in range(tracers):
        total = jnp.zeros((8, 128), F32)
        for s in range(cells_ref.shape[0]):
            total = total + jnp.where(cell == cells_ref[s], weights_ref[t, s], 0.0)
        top = pl.ds(t * levels * 8, 8)
        started_ref[top, :] = field_ref[top, :] + total
    rows_out(started_ref, up_ref, down_ref)
    columns_out(started_ref, east_ref, west_ref, levels)

    def group(g, carry):
        below, inverse = carry
        for j in range(GROUP):
            spot = pl.ds((g * GROUP + j) * 8, 8)
            here = diffusion_ref[spot, :]
            inverse = 1.0 / (1.0 + below + here - below * below * inverse)
            inverse_ref[spot, :] = inverse
            below = here
        return below, inverse

    zero = jnp.zeros((8, 128), F32)
    lax.fori_loop(0, levels // GROUP, group, (zero, zero))


def step_body(field_ref, u_ref, v_ref, k_ref, inverse_ref, low, high, west, east, out_ref):
    levels = k_ref.shape[0] // 8
    tracers = field_ref.shape[0] // (8 * levels)
    lane = lanes_iota()
    row = rows_iota()
    last_lane, first_lane = lane == 127, lane == 0
    last_row, first_row = row == 7, row == 0
    zero = jnp.zeros((8, 128), F32)

    def forward(g, carry):
        below, state = carry[0], list(carry[1])
        for j in range(GROUP):
            level = g * GROUP + j
            spot = pl.ds(level * 8, 8)
            u, v = u_ref[spot, :], v_ref[spot, :]
            inverse = inverse_ref[spot, :]
            lift = below * inverse
            to_east = jnp.maximum(u, 0.0) * inverse
            to_west = jnp.maximum(-u, 0.0) * inverse
            to_north = jnp.maximum(v, 0.0) * inverse
            to_south = jnp.maximum(-v, 0.0) * inverse
            centre = inverse - jnp.abs(u) * inverse - jnp.abs(v) * inverse
            for t in range(tracers):
                at = t * levels + level
                x = field_ref[pl.ds(at * 8, 8), :]
                xe = jnp.where(
                    last_lane, pltpu.roll(east[t], 127 - level, 1), pltpu.roll(x, 127, 1)
                )
                xw = jnp.where(
                    first_lane, pltpu.roll(west[t], 128 - level, 1), pltpu.roll(x, 1, 1)
                )
                xn = jnp.where(last_row, high[pl.ds(at, 1), :], pltpu.roll(x, 7, 0))
                xs = jnp.where(first_row, low[pl.ds(at, 1), :], pltpu.roll(x, 1, 0))
                q = centre * x + to_east * xe + to_west * xw + to_north * xn + to_south * xs
                state[t] = q + lift * state[t]
                out_ref[pl.ds(at * 8, 8), :] = state[t]
            below = k_ref[spot, :]
        return below, tuple(state)

    lax.fori_loop(0, levels // GROUP, forward, (zero, (zero,) * tracers))

    def backward(g, state):
        state = list(state)
        for j in range(GROUP):
            level = levels - 1 - g * GROUP - j
            spot = pl.ds(level * 8, 8)
            upper = k_ref[spot, :] * inverse_ref[spot, :]
            for t in range(tracers):
                here = pl.ds((t * levels + level) * 8, 8)
                state[t] = out_ref[here, :] + upper * state[t]
                out_ref[here, :] = state[t]
        return tuple(state)

    lax.fori_loop(0, levels // GROUP, backward, (zero,) * tracers)


def step_kernel(
    field_ref,
    u_ref,
    v_ref,
    k_ref,
    inverse_ref,
    low_ref,
    high_ref,
    west_ref,
    east_ref,
    out_ref,
    *edge_refs,
):
    step_body(
        field_ref, u_ref, v_ref, k_ref, inverse_ref, low_ref, high_ref, west_ref, east_ref, out_ref
    )
    if edge_refs:
        up_ref, down_ref, east_out, west_out = edge_refs
        rows_out(out_ref, up_ref, down_ref)
        columns_out(out_ref, east_out, west_out, k_ref.shape[0] // 8)


def inject_kernel(received_ref, first_ref, out_ref, up_ref, down_ref, east_ref, west_ref):
    sources = received_ref.shape[0]
    tracers = east_ref.shape[0]
    levels = first_ref.shape[0] // (8 * tracers)
    rows = jnp.concatenate([received_ref[s, 0:levels, :] for s in range(sources)], axis=1)
    tail = jnp.concatenate([received_ref[s, 64:80, :] for s in range(sources)], axis=1).astype(F32)
    misfit = [tail[8 + t : 9 + t, :].astype(BF16) for t in range(tracers)]
    cell_row = tail[12:13, :]
    cell_lane = tail[13:14, :].astype(BF16)
    width = sources * 128
    lane = lax.broadcasted_iota(jnp.int32, (128, width), 0).astype(F32).astype(BF16)
    hot = jnp.where(lane == cell_lane, jnp.ones((), BF16), jnp.zeros((), BF16))
    for r in range(8):
        here = jnp.where(cell_row == r, 1.0, 0.0).astype(BF16)
        weighted = jnp.concatenate([hot * (here * misfit[t]) for t in range(tracers)], axis=0)
        forcing = lax.dot_general(
            rows, weighted, (((1,), (1,)), ((), ())), preferred_element_type=F32
        )
        for t in range(tracers):
            spot = pl.ds(t * levels * 8 + r, levels, stride=8)
            out_ref[spot, :] = first_ref[spot, :] + forcing[:, t * 128 : (t + 1) * 128]
    rows_out(out_ref, up_ref, down_ref)
    columns_out(out_ref, east_ref, west_ref, levels)


def exchange(edges):
    up, down, east, west = edges
    lat, lon = lax.axis_size("lat"), lax.axis_size("lon")
    north = [(i, i + 1) for i in range(lat - 1)]
    right = [(i, (i + 1) % lon) for i in range(lon)]
    low = lax.ppermute(up, "lat", north)
    high = lax.ppermute(down, "lat", [(b, a) for a, b in north])
    from_west = lax.ppermute(east, "lon", right)
    from_east = lax.ppermute(west, "lon", [(b, a) for a, b in right])
    return low, high, from_west, from_east


def body(
    adjoint_in,
    wind_u,
    wind_v,
    diffusion,
    kernel_rows,
    retrieval_misfit,
    retrieval_columns,
    retrieval_counts,
    station_cells,
    station_misfit,
):
    tracers, levels, lat_rows, lon_cells = adjoint_in.shape
    slots = kernel_rows.shape[1]
    tiles = lax.axis_size("lon")
    smem = pl.BlockSpec(memory_space=pltpu.SMEM)
    vmem = pl.BlockSpec(memory_space=pltpu.VMEM)
    call = functools.partial(pl.pallas_call, compiler_params=PARAMS)
    full = jax.ShapeDtypeStruct((tracers * levels * 8, 128), F32)
    planes = jax.ShapeDtypeStruct((levels * 8, 128), F32)
    edge_row = jax.ShapeDtypeStruct((tracers * levels, 128), F32)
    edge_column = jax.ShapeDtypeStruct((tracers, 8, 128), F32)
    edges = (edge_row, edge_row, edge_column, edge_column)

    packed = call(
        pack_kernel,
        out_shape=jax.ShapeDtypeStruct((tiles, 80, 128), BF16),
        in_specs=[smem, vmem, vmem, vmem],
        name="pack",
    )(retrieval_counts, kernel_rows, retrieval_misfit, retrieval_columns.reshape(slots // 128, 128))
    received = lax.all_to_all(packed, "lon", split_axis=0, concat_axis=0, tiled=True)

    field = adjoint_in.reshape(full.shape)
    u = wind_u.reshape(planes.shape)
    v = wind_v.reshape(planes.shape)
    k = diffusion.reshape(planes.shape)
    started, inverse, *sent = call(
        prep_kernel,
        out_shape=(full, planes) + edges,
        in_specs=[smem, smem, vmem, vmem],
        name="prep",
    )(station_cells, station_misfit, field, k)
    first = call(step_kernel, out_shape=full, name="first")(
        started, u, v, k, inverse, *exchange(sent)
    )
    injected, *sent = call(inject_kernel, out_shape=(full,) + edges, name="inject")(received, first)
    second, *sent = call(step_kernel, out_shape=(full,) + edges, name="second")(
        injected, u, v, k, inverse, *exchange(sent)
    )
    last = call(step_kernel, out_shape=full, name="last")(
        second, u, v, k, inverse, *exchange(sent)
    )
    return last.reshape(adjoint_in.shape)


def solution(mesh):
    return jax.shard_map(
        body,
        mesh=mesh,
        in_specs=(
            P(None, None, "lat", "lon"),
            P(None, "lat", "lon"),
            P(None, "lat", "lon"),
            P(None, "lat", "lon"),
            P(None, ("lat", "lon")),
            P(None, ("lat", "lon")),
            P(("lat", "lon")),
            P(("lat", "lon")),
            P(("lat", "lon")),
            P(None, ("lat", "lon")),
        ),
        out_specs=P(None, None, "lat", "lon"),
        check_vma=False,
    )
```

```python
import jax
import jax.numpy as jnp
from jax import lax
from jax.experimental import pallas as pl
from jax.experimental.pallas import tpu as pltpu
from jax.sharding import PartitionSpec as P

F32 = jnp.float32
BF16 = jnp.bfloat16
GROUP = 8


def vmem_call(kernel, *, out_shape, smem=0, scratch=(), limit=16, name):
    is_tuple = isinstance(out_shape, tuple)
    outs = out_shape if is_tuple else (out_shape,)
    outs = tuple(pltpu.VMEM(o.shape, o.dtype) for o in outs)

    def run(*args):
        args = args[:smem] + tuple(
            pltpu.with_memory_space_constraint(a, pltpu.VMEM) for a in args[smem:]
        )
        specs = [pl.BlockSpec(memory_space=pltpu.SMEM)] * smem
        specs += [pl.BlockSpec(memory_space=pltpu.VMEM)] * (len(args) - smem)
        return pl.pallas_call(
            kernel,
            out_shape=outs if is_tuple else outs[0],
            in_specs=specs,
            scratch_shapes=[pltpu.VMEM(o.shape, o.dtype) for o in scratch],
            compiler_params=pltpu.CompilerParams(vmem_limit_bytes=limit << 20),
            name=name,
        )(*args)

    return run


def lanes_iota():
    return lax.broadcasted_iota(jnp.int32, (8, 128), 1)


def rows_iota():
    return lax.broadcasted_iota(jnp.int32, (8, 128), 0)


def pack_kernel(count_ref, rows_ref, misfit_ref, columns_ref, out_ref):
    chunks = columns_ref.shape[0]
    tiles = out_ref.shape[0]
    count = count_ref[0]
    lane = lax.broadcasted_iota(jnp.int32, (1, 128), 1)
    tile = lax.broadcasted_iota(jnp.int32, (tiles, 128), 0)
    hits = []
    targets = []
    misc = []
    for j in range(chunks):
        column = columns_ref[j : j + 1, :]
        live = (lane + j * 128) < count
        target = jnp.where(live, column >> 10, -1)
        targets.append(target)
        hits.append((tile == target).astype(F32))
        cell = column & 1023
        misc.append(
            jnp.concatenate(
                [
                    misfit_ref[:, j * 128 : (j + 1) * 128].astype(F32),
                    (cell >> 7).astype(F32),
                    (cell & 127).astype(F32),
                    jnp.zeros((2, 128), F32),
                ],
                axis=0,
            )
        )
    before = lax.broadcasted_iota(jnp.int32, (128, 128), 0) < lax.broadcasted_iota(
        jnp.int32, (128, 128), 1
    )
    prefix = jnp.dot(
        jnp.concatenate(hits, axis=0).astype(BF16),
        before.astype(F32).astype(BF16),
        preferred_element_type=F32,
    )
    offset = jnp.zeros((tiles, 1), F32)
    ranks = []
    for j in range(chunks):
        rank = jnp.sum(
            hits[j] * (prefix[j * tiles : (j + 1) * tiles] + offset), axis=0, keepdims=True
        )
        ranks.append(rank)
        offset = offset + jnp.sum(hits[j], axis=1, keepdims=True)
    tail = jnp.concatenate(
        [rows_ref[64:72, :].astype(F32), jnp.concatenate(misc, axis=1)], axis=0
    ).astype(BF16)
    payload = jnp.concatenate([rows_ref[0:64, :], tail], axis=0)
    rank = jnp.concatenate(ranks, axis=0).T
    target = jnp.concatenate(targets, axis=0).astype(F32).T
    slot = lax.broadcasted_iota(jnp.int32, (128, 128), 1).astype(F32).astype(BF16)
    one, zero = jnp.ones((), BF16), jnp.zeros((), BF16)
    spread = [
        [jnp.broadcast_to(x[:, j : j + 1], (128, 128)).astype(BF16) for j in range(chunks)]
        for x in (rank, target)
    ]
    hot = jnp.concatenate([jnp.where(x == slot, one, zero) for x in spread[0]], axis=0)
    target = jnp.concatenate(spread[1], axis=0)
    for pair in range(tiles // 2):
        chosen = [
            jnp.where(target == jnp.asarray(2.0 * pair + side, BF16), hot, zero)
            for side in range(2)
        ]
        packed = jnp.dot(
            payload, jnp.concatenate(chosen, axis=1), preferred_element_type=F32
        ).astype(BF16)
        out_ref[2 * pair] = packed[:, :128]
        out_ref[2 * pair + 1] = packed[:, 128:]


def add_column(total, x, source, target, width):
    lane = lanes_iota()
    here = (lane >= target) & (lane < target + width)
    return jnp.where(here, pltpu.roll(x, (target - source + 128) % 128, 1), total)


def prep_kernel(
    cells_ref,
    weights_ref,
    field_ref,
    u_ref,
    v_ref,
    k_ref,
    surface_ref,
    up_ref,
    down_ref,
    east_ref,
    west_ref,
):
    levels = k_ref.shape[0] // 8
    tracers = field_ref.shape[0] // (8 * levels)
    cell = rows_iota() * 128 + lanes_iota()
    surface = []
    for t in range(tracers):
        total = jnp.zeros((8, 128), F32)
        for s in range(cells_ref.shape[0]):
            total = total + jnp.where(cell == cells_ref[s], weights_ref[t, s], 0.0)
        surface.append(total)
        surface_ref[t] = total
    count = tracers * levels
    for row, ref in ((7, up_ref), (0, down_ref)):
        ref[0:count, :] = field_ref[pl.ds(row, count, stride=8), :]
        for t in range(tracers):
            top = slice(t * levels, t * levels + 1)
            ref[top, :] = ref[top, :] + surface[t][row : row + 1, :]
        for i, plane in enumerate((u_ref, v_ref, k_ref)):
            at = count + i * levels
            ref[at : at + levels, :] = plane[pl.ds(row, levels, stride=8), :]

    def group(g, carry):
        east, west = list(carry[0]), list(carry[1])
        for j in range(GROUP):
            level = g * GROUP + j
            spot = pl.ds(level * 8, 8)
            values = [field_ref[pl.ds((t * levels + level) * 8, 8), :] for t in range(tracers)]
            if j == 0:
                values = [x + jnp.where(g == 0, add, 0.0) for x, add in zip(values, surface)]
            values += [u_ref[spot, :], v_ref[spot, :], k_ref[spot, :]]
            for i, x in enumerate(values):
                east[i] = add_column(east[i], x, 127, level, 1)
                west[i] = add_column(west[i], x, 0, level, 1)
        return tuple(east), tuple(west)

    zeros = (jnp.zeros((8, 128), F32),) * (tracers + 3)
    east, west = lax.fori_loop(0, levels // GROUP, group, (zeros, zeros))
    for i in range(tracers + 3):
        east_ref[i] = east[i]
        west_ref[i] = west[i]


def factor_kernel(k_ref, inverse_ref):
    def group(g, carry):
        below, inverse = carry
        for j in range(GROUP):
            spot = pl.ds((g * GROUP + j) * 8, 8)
            here = k_ref[spot, :]
            inverse = 1.0 / (1.0 + below + here - below * below * inverse)
            inverse_ref[spot, :] = inverse
            below = here
        return below, inverse

    zero = jnp.zeros((8, 128), F32)
    lax.fori_loop(0, k_ref.shape[0] // (8 * GROUP), group, (zero, zero))


class Advection:
    def __init__(self, u, v, inverse, below):
        self.lift = below * inverse
        self.east = jnp.maximum(u, 0.0) * inverse
        self.west = jnp.maximum(-u, 0.0) * inverse
        self.north = jnp.maximum(v, 0.0) * inverse
        self.south = jnp.maximum(-v, 0.0) * inverse
        self.centre = inverse - jnp.abs(u) * inverse - jnp.abs(v) * inverse

    def __call__(self, x, east, west, north, south):
        return (
            self.centre * x
            + self.east * east
            + self.west * west
            + self.north * north
            + self.south * south
        )


def shifted(x, east, west, north, south):
    lane, row = lanes_iota(), rows_iota()
    return (
        jnp.where(lane == 127, east, pltpu.roll(x, 127, 1)),
        jnp.where(lane == 0, west, pltpu.roll(x, 1, 1)),
        jnp.where(row == 7, north, pltpu.roll(x, 7, 0)),
        jnp.where(row == 0, south, pltpu.roll(x, 1, 0)),
    )


def first_kernel(
    field_ref,
    surface_ref,
    u_ref,
    v_ref,
    k_ref,
    inverse_ref,
    forcing_ref,
    low_ref,
    high_ref,
    west_ref,
    east_ref,
    out_ref,
    up_ref,
    down_ref,
):
    levels = k_ref.shape[0] // 8
    tracers = field_ref.shape[0] // (8 * levels)
    zero = jnp.zeros((8, 128), F32)
    east = [east_ref[t] for t in range(tracers)]
    west = [west_ref[t] for t in range(tracers)]

    def forward(g, carry):
        below, state = carry[0], list(carry[1])
        for j in range(GROUP):
            level = g * GROUP + j
            spot = pl.ds(level * 8, 8)
            advect = Advection(u_ref[spot, :], v_ref[spot, :], inverse_ref[spot, :], below)
            for t in range(tracers):
                at = t * levels + level
                x = field_ref[pl.ds(at * 8, 8), :]
                if j == 0:
                    x = x + jnp.where(g == 0, surface_ref[t], 0.0)
                around = shifted(
                    x,
                    pltpu.roll(east[t], 127 - level, 1),
                    pltpu.roll(west[t], 128 - level, 1),
                    high_ref[pl.ds(at, 1), :],
                    low_ref[pl.ds(at, 1), :],
                )
                state[t] = advect(x, *around) + advect.lift * state[t]
                out_ref[pl.ds(at * 8, 8), :] = state[t]
            below = k_ref[spot, :]
        return below, tuple(state)

    lax.fori_loop(0, levels // GROUP, forward, (zero, (zero,) * tracers))
    back(levels, tracers, k_ref, inverse_ref, out_ref, (), forcing_ref)
    count = tracers * levels
    lane, row = lanes_iota(), rows_iota()
    for ref, near, far in ((up_ref, 7, 6), (down_ref, 0, 1)):
        ref[0:count, :] = out_ref[pl.ds(near, count, stride=8), :]
        ref[count : 2 * count, :] = out_ref[pl.ds(far, count, stride=8), :]
        for at, source in ((2 * count, 126), (2 * count + 8, 0)):
            ref[at : at + 8, :] = zero
            for part in range((levels + 15) // 16):
                total = zero
                for start in range(16 * part, min(16 * part + 16, levels), 8):
                    for t in range(tracers):
                        x = ref[t * levels + start : t * levels + start + 8, :]
                        target = start % 16 * 8 + 2 * t
                        x = pltpu.roll(
                            x, (target - source + 128) % 128, 1, stride=8, stride_axis=0
                        )
                        total = jnp.where((lane - target - 8 * row) >> 1 == 0, x, total)
                ref[at + part : at + part + 1, :] = jnp.sum(total, axis=0, keepdims=True)


def back(levels, tracers, k_ref, inverse_ref, out_ref, others, added_ref=None):
    zero = jnp.zeros((8, 128), F32)

    def group(g, state):
        state = list(state)
        for j in range(GROUP):
            level = levels - 1 - g * GROUP - j
            spot = pl.ds(level * 8, 8)
            upper = k_ref[spot, :] * inverse_ref[spot, :]
            for t in range(tracers):
                here = pl.ds((t * levels + level) * 8, 8)
                state[t] = out_ref[here, :] + upper * state[t]
                if added_ref is None:
                    out_ref[here, :] = state[t]
                else:
                    out_ref[here, :] = state[t] + added_ref[here, :]
            for i, (ref, k, inverse) in enumerate(others):
                i += tracers
                state[i] = ref[spot, :] + k[spot, :] * inverse[spot, :] * state[i]
                ref[spot, :] = state[i]
        return tuple(state)

    lax.fori_loop(0, levels // GROUP, group, (zero,) * (tracers + len(others)))


def ring_kernel(
    low_ref, high_ref, west_ref, east_ref, u_ref, v_ref, k_ref, inverse_ref, *column_refs
):
    column_u_ref, column_v_ref, column_k_ref, column_inverse_ref = column_refs
    levels = u_ref.shape[0] // 8
    tracers = (low_ref.shape[0] - 3 * levels) // levels
    above = rows_iota() < tracers
    lane = lanes_iota()
    even = (lane & 1) == 0
    east = [east_ref[tracers + i] for i in range(3)]
    west = [west_ref[tracers + i] for i in range(3)]
    zero = jnp.zeros((8, 128), F32)
    column_u_ref[...] = jnp.zeros_like(column_u_ref)
    column_v_ref[...] = jnp.zeros_like(column_v_ref)
    below, inverse, column_below, column_inverse = zero, zero, zero, zero
    for level in range(levels):
        spot = pl.ds(level * 8, 8)
        at = [tracers * levels + i * levels + level for i in range(3)]
        u, v, k = (
            jnp.where(above, high_ref[pl.ds(i, 1), :], low_ref[pl.ds(i, 1), :]) for i in at
        )
        u_ref[spot, :] = u
        v_ref[spot, :] = jnp.where(above, v, -v)
        k_ref[spot, :] = k
        inverse = 1.0 / (1.0 + below + k - below * below * inverse)
        inverse_ref[spot, :] = inverse
        below = k
        u, v, k = (
            jnp.where(
                even,
                jnp.broadcast_to(e[:, level : level + 1], (8, 128)),
                jnp.broadcast_to(w[:, level : level + 1], (8, 128)),
            )
            for e, w in zip(east, west)
        )
        column_k_ref[spot, :] = k
        column_inverse = 1.0 / (1.0 + column_below + k - column_below * column_below * column_inverse)
        column_inverse_ref[spot, :] = column_inverse
        column_below = k
        packed = pl.ds(level // 16 * 8, 8)
        here = (lane >> 3) == level % 16
        column_u_ref[packed, :] = jnp.where(here, jnp.where(even, u, -u), column_u_ref[packed, :])
        column_v_ref[packed, :] = jnp.where(here, v, column_v_ref[packed, :])


def forcing_kernel(received_ref, out_ref):
    sources = received_ref.shape[0]
    levels = 72
    tracers = out_ref.shape[0] // (8 * levels)
    count = tracers * levels
    rows = jnp.concatenate([received_ref[s, 0:levels, :] for s in range(sources)], axis=1)
    rows = rows.astype(F32)
    tail = jnp.concatenate([received_ref[s, 64:80, :] for s in range(sources)], axis=1).astype(F32)
    high, low = [], []
    for t in range(tracers):
        product = rows * tail[8 + t : 9 + t, :]
        high.append(product.astype(BF16))
        low.append((product - high[t].astype(F32)).astype(BF16))
    products = jnp.concatenate(high + low, axis=0)
    cell_row = tail[12:13, :]
    cell_lane = tail[13:14, :].astype(BF16)
    lane = lax.broadcasted_iota(jnp.int32, (128, sources * 128), 0).astype(F32).astype(BF16)
    hot = jnp.where(lane == cell_lane, jnp.ones((), BF16), jnp.zeros((), BF16))
    for r in range(0, 8, 2):
        cells = jnp.concatenate(
            [hot * jnp.where(cell_row == r + i, 1.0, 0.0).astype(BF16) for i in range(2)], axis=0
        )
        both = lax.dot_general(
            products, cells, (((1,), (1,)), ((), ())), preferred_element_type=F32
        )
        both = both[:count] + both[count:]
        for i in range(2):
            out_ref[pl.ds(r + i, count, stride=8), :] = both[:, i * 128 : (i + 1) * 128]


def columns_kernel(field_ref, east_ref, west_ref):
    levels = 72
    tracers = field_ref.shape[0] // (8 * levels)
    for part in range(east_ref.shape[0] // 8):
        east = jnp.zeros((8, 128), F32)
        west = jnp.zeros((8, 128), F32)
        for level in range(16 * part, min(16 * part + 16, levels)):
            for t in range(tracers):
                x = field_ref[pl.ds((t * levels + level) * 8, 8), :]
                target = level % 16 * 8 + 2 * t
                east = add_column(east, x, 126, target, 2)
                west = add_column(west, x, 0, target, 2)
        east_ref[part * 8 : part * 8 + 8, :] = east
        west_ref[part * 8 : part * 8 + 8, :] = west


def relay_kernel(low_ref, high_ref, east_ref, west_ref, east_out, west_out):
    rows = east_ref.shape[0]
    corner = low_ref.shape[0] - 16
    for out, ref, at in ((east_out, east_ref, corner), (west_out, west_ref, corner + 8)):
        out[0:rows, :] = ref[...]
        out[rows : rows + 8, :] = high_ref[at : at + 8, :]
        out[rows + 8 : rows + 16, :] = low_ref[at : at + 8, :]


def last_kernel(
    field_ref,
    u_ref,
    v_ref,
    k_ref,
    inverse_ref,
    low_ref,
    high_ref,
    west_ref,
    east_ref,
    own_west_ref,
    own_east_ref,
    ring_u_ref,
    ring_v_ref,
    ring_k_ref,
    ring_inverse_ref,
    column_u_ref,
    column_v_ref,
    column_k_ref,
    column_inverse_ref,
    out_ref,
    middle_ref,
    near_ref,
    far_ref,
    inner_ref,
    ring_ref,
    packed_ref,
    column_ref,
):
    levels = k_ref.shape[0] // 8
    tracers = field_ref.shape[0] // (8 * levels)
    count = tracers * levels
    parts = own_east_ref.shape[0] // 8
    lane, row = lanes_iota(), rows_iota()
    even = (lane & 1) == 0
    above = row < tracers
    zero = jnp.zeros((8, 128), F32)
    for t in range(tracers):
        for side, (ref, edge) in enumerate(((high_ref, 7), (low_ref, 0))):
            spot = pl.ds(side * tracers + t, levels, stride=8)
            at = t * levels
            near_ref[spot, :] = ref[at : at + levels, :]
            far_ref[spot, :] = ref[count + at : count + at + levels, :]
            inner_ref[spot, :] = field_ref[pl.ds(at * 8 + edge, levels, stride=8), :]
    for part in range(parts):
        spot = pl.ds(part * 8, 8)
        east, west = east_ref[spot, :], west_ref[spot, :]
        x = jnp.where(even, east, west)
        outer = jnp.where(even, pltpu.roll(east, 127, 1), pltpu.roll(west, 1, 1))
        inner = jnp.where(
            even, pltpu.roll(own_east_ref[spot, :], 127, 1), pltpu.roll(own_west_ref[spot, :], 1, 1)
        )
        ends = [
            jnp.where(
                even,
                jnp.broadcast_to(east_ref[pl.ds(at, 1), :], (8, 128)),
                jnp.broadcast_to(west_ref[pl.ds(at, 1), :], (8, 128)),
            )
            for at in (parts * 8 + part, parts * 8 + 8 + part)
        ]
        north = jnp.where(row == 7, ends[0], pltpu.roll(x, 7, 0))
        south = jnp.where(row == 0, ends[1], pltpu.roll(x, 1, 0))
        advect = Advection(column_u_ref[spot, :], column_v_ref[spot, :], zero + 1.0, zero)
        packed_ref[spot, :] = advect(x, outer, inner, north, south)

    def forward(g, carry):
        below, ring_below, column_below = carry[0]
        state = list(carry[1])
        part = g * GROUP // 16
        east = east_ref[pl.ds(part * 8, 8), :]
        west = west_ref[pl.ds(part * 8, 8), :]
        corner_east, corner_west = (
            jnp.where(
                above,
                jnp.broadcast_to(ref[pl.ds(parts * 8 + part, 1), :], (8, 128)),
                jnp.broadcast_to(ref[pl.ds(parts * 8 + 8 + part, 1), :], (8, 128)),
            )
            for ref in (east_ref, west_ref)
        )
        packed = packed_ref[pl.ds(part * 8, 8), :]
        for j in range(GROUP):
            level = g * GROUP + j
            start = (level % 16) * 8
            spot = pl.ds(level * 8, 8)
            advect = Advection(u_ref[spot, :], v_ref[spot, :], inverse_ref[spot, :], below)
            for t in range(tracers):
                here = pl.ds((t * levels + level) * 8, 8)
                x = field_ref[here, :]
                around = shifted(
                    x,
                    pltpu.roll(east, 127 - start - 2 * t, 1),
                    pltpu.roll(west, 127 - start - 2 * t, 1),
                    near_ref[pl.ds(level * 8 + t, 1), :],
                    near_ref[pl.ds(level * 8 + tracers + t, 1), :],
                )
                state[t] = advect(x, *around) + advect.lift * state[t]
                middle_ref[here, :] = state[t]
            x = near_ref[spot, :]
            mine = start + 2 * (row % tracers)
            end_east = jnp.sum(jnp.where(lane == mine, corner_east, 0.0), axis=1, keepdims=True)
            end_west = jnp.sum(jnp.where(lane == mine + 1, corner_west, 0.0), axis=1, keepdims=True)
            advect = Advection(
                ring_u_ref[spot, :], ring_v_ref[spot, :], ring_inverse_ref[spot, :], ring_below
            )
            state[tracers] = (
                advect(
                    x,
                    jnp.where(lane == 127, end_east, pltpu.roll(x, 127, 1)),
                    jnp.where(lane == 0, end_west, pltpu.roll(x, 1, 1)),
                    far_ref[spot, :],
                    inner_ref[spot, :],
                )
                + advect.lift * state[tracers]
            )
            ring_ref[spot, :] = state[tracers]
            column_inverse = column_inverse_ref[spot, :]
            state[tracers + 1] = (
                pltpu.roll(packed, 128 - start, 1) * column_inverse
                + column_below * column_inverse * state[tracers + 1]
            )
            column_ref[spot, :] = state[tracers + 1]
            below, ring_below, column_below = (
                k_ref[spot, :],
                ring_k_ref[spot, :],
                column_k_ref[spot, :],
            )
        return (below, ring_below, column_below), tuple(state)

    lax.fori_loop(
        0, levels // GROUP, forward, ((zero, zero, zero), (zero,) * (tracers + 2))
    )
    back(
        levels,
        tracers,
        k_ref,
        inverse_ref,
        middle_ref,
        (
            (ring_ref, ring_k_ref, ring_inverse_ref),
            (column_ref, column_k_ref, column_inverse_ref),
        ),
    )

    def final(g, carry):
        below, state = carry[0], list(carry[1])
        for j in range(GROUP):
            level = g * GROUP + j
            spot = pl.ds(level * 8, 8)
            advect = Advection(u_ref[spot, :], v_ref[spot, :], inverse_ref[spot, :], below)
            sides = column_ref[spot, :]
            for t in range(tracers):
                here = pl.ds((t * levels + level) * 8, 8)
                x = middle_ref[here, :]
                around = shifted(
                    x,
                    pltpu.roll(sides, 127 - 2 * t, 1),
                    pltpu.roll(sides, 127 - 2 * t, 1),
                    ring_ref[pl.ds(level * 8 + t, 1), :],
                    ring_ref[pl.ds(level * 8 + tracers + t, 1), :],
                )
                state[t] = advect(x, *around) + advect.lift * state[t]
                out_ref[here, :] = state[t]
            below = k_ref[spot, :]
        return below, tuple(state)

    lax.fori_loop(0, levels // GROUP, final, (zero, (zero,) * tracers))
    back(levels, tracers, k_ref, inverse_ref, out_ref, ())


def to_rows(up, down):
    lat = lax.axis_size("lat")
    north = [(i, i + 1) for i in range(lat - 1)]
    return lax.ppermute(up, "lat", north), lax.ppermute(down, "lat", [(b, a) for a, b in north])


def to_columns(east, west):
    lon = lax.axis_size("lon")
    right = [(i, (i + 1) % lon) for i in range(lon)]
    return lax.ppermute(east, "lon", right), lax.ppermute(west, "lon", [(b, a) for a, b in right])


def body(
    adjoint_in,
    wind_u,
    wind_v,
    diffusion,
    kernel_rows,
    retrieval_misfit,
    retrieval_columns,
    retrieval_counts,
    station_cells,
    station_misfit,
):
    tracers, levels, lat_rows, lon_cells = adjoint_in.shape
    slots = kernel_rows.shape[1]
    tiles = lax.axis_size("lon")
    parts = (levels + 15) // 16
    full = jax.ShapeDtypeStruct((tracers * levels * 8, 128), F32)
    planes = jax.ShapeDtypeStruct((levels * 8, 128), F32)
    rows_one = jax.ShapeDtypeStruct(((tracers + 3) * levels, 128), F32)
    columns_one = jax.ShapeDtypeStruct((tracers + 3, 8, 128), F32)
    rows_two = jax.ShapeDtypeStruct((2 * tracers * levels + 16, 128), F32)
    columns_two = jax.ShapeDtypeStruct((parts * 8, 128), F32)
    columns_sent = jax.ShapeDtypeStruct((parts * 8 + 16, 128), F32)

    packed = pl.pallas_call(
        pack_kernel,
        out_shape=jax.ShapeDtypeStruct((tiles, 80, 128), BF16),
        in_specs=[pl.BlockSpec(memory_space=pltpu.SMEM)]
        + [pl.BlockSpec(memory_space=pltpu.VMEM)] * 3,
        compiler_params=pltpu.CompilerParams(vmem_limit_bytes=56 << 20),
        name="pack",
    )(retrieval_counts, kernel_rows, retrieval_misfit, retrieval_columns.reshape(slots // 128, 128))
    received = lax.all_to_all(packed, "lon", split_axis=0, concat_axis=0, tiled=True)

    field = adjoint_in.reshape(full.shape)
    u = wind_u.reshape(planes.shape)
    v = wind_v.reshape(planes.shape)
    k = diffusion.reshape(planes.shape)
    surface, up, down, east, west = vmem_call(
        prep_kernel,
        out_shape=(
            jax.ShapeDtypeStruct((tracers, 8, 128), F32),
            rows_one,
            rows_one,
            columns_one,
            columns_one,
        ),
        smem=2,
        name="prep",
    )(station_cells, station_misfit, field, u, v, k)
    low, high = to_rows(up, down)
    from_west, from_east = to_columns(east, west)
    inverse = vmem_call(factor_kernel, out_shape=planes, name="factor")(k)
    ring = vmem_call(
        ring_kernel,
        out_shape=(planes,) * 4 + (columns_two,) * 2 + (planes,) * 2,
        name="ring",
    )(low, high, from_west, from_east)
    forcing = vmem_call(forcing_kernel, out_shape=full, limit=30, name="forcing")(received)
    injected, up, down = vmem_call(
        first_kernel, out_shape=(full, rows_two, rows_two), name="first"
    )(field, surface, u, v, k, inverse, forcing, low, high, from_west, from_east)
    east, west = vmem_call(columns_kernel, out_shape=(columns_two,) * 2, name="columns")(injected)
    low, high = to_rows(up, down)
    sent = vmem_call(relay_kernel, out_shape=(columns_sent,) * 2, name="relay")(
        low, high, east, west
    )
    from_west, from_east = to_columns(*sent)
    last = vmem_call(
        last_kernel,
        out_shape=full,
        scratch=(full,) + (planes,) * 4 + (columns_two, planes),
        name="last",
    )(injected, u, v, k, inverse, low, high, from_west, from_east, west, east, *ring)
    return last.reshape(adjoint_in.shape)


def solution(mesh):
    return jax.shard_map(
        body,
        mesh=mesh,
        in_specs=(
            P(None, None, "lat", "lon"),
            P(None, "lat", "lon"),
            P(None, "lat", "lon"),
            P(None, "lat", "lon"),
            P(None, ("lat", "lon")),
            P(None, ("lat", "lon")),
            P(("lat", "lon")),
            P(("lat", "lon")),
            P(("lat", "lon")),
            P(None, ("lat", "lon")),
        ),
        out_specs=P(None, None, "lat", "lon"),
        check_vma=False,
    )
```

```python
import jax
import jax.numpy as jnp
from jax import lax
from jax.experimental import pallas as pl
from jax.experimental.pallas import tpu as pltpu
from jax.sharding import PartitionSpec as P

F32 = jnp.float32
BF16 = jnp.bfloat16
GROUP = 72


def vmem_call(kernel, *, out_shape, smem=0, scratch=(), limit=16, name):
    is_tuple = isinstance(out_shape, tuple)
    outs = out_shape if is_tuple else (out_shape,)
    outs = tuple(pltpu.VMEM(o.shape, o.dtype) for o in outs)

    def run(*args):
        args = args[:smem] + tuple(
            pltpu.with_memory_space_constraint(a, pltpu.VMEM) for a in args[smem:]
        )
        specs = [pl.BlockSpec(memory_space=pltpu.SMEM)] * smem
        specs += [pl.BlockSpec(memory_space=pltpu.VMEM)] * (len(args) - smem)
        return pl.pallas_call(
            kernel,
            out_shape=outs if is_tuple else outs[0],
            in_specs=specs,
            scratch_shapes=[pltpu.VMEM(o.shape, o.dtype) for o in scratch],
            compiler_params=pltpu.CompilerParams(vmem_limit_bytes=limit << 20),
            name=name,
        )(*args)

    return run


def lanes_iota():
    return lax.broadcasted_iota(jnp.int32, (8, 128), 1)


def rows_iota():
    return lax.broadcasted_iota(jnp.int32, (8, 128), 0)


def pack_kernel(count_ref, rows_ref, misfit_ref, columns_ref, out_ref):
    chunks = columns_ref.shape[0]
    tiles = out_ref.shape[0]
    count = count_ref[0]
    lane = lax.broadcasted_iota(jnp.int32, (1, 128), 1)
    tile = lax.broadcasted_iota(jnp.int32, (tiles, 128), 0)
    hits = []
    targets = []
    misc = []
    for j in range(chunks):
        column = columns_ref[j : j + 1, :]
        live = (lane + j * 128) < count
        target = jnp.where(live, column >> 10, -1)
        targets.append(target)
        hits.append((tile == target).astype(F32))
        cell = column & 1023
        misc.append(
            jnp.concatenate(
                [
                    misfit_ref[:, j * 128 : (j + 1) * 128].astype(F32),
                    (cell >> 7).astype(F32),
                    (cell & 127).astype(F32),
                    jnp.zeros((2, 128), F32),
                ],
                axis=0,
            )
        )
    before = lax.broadcasted_iota(jnp.int32, (128, 128), 0) < lax.broadcasted_iota(
        jnp.int32, (128, 128), 1
    )
    prefix = jnp.dot(
        jnp.concatenate(hits, axis=0).astype(BF16),
        before.astype(F32).astype(BF16),
        preferred_element_type=F32,
    )
    offset = jnp.zeros((tiles, 1), F32)
    ranks = []
    for j in range(chunks):
        rank = jnp.sum(
            hits[j] * (prefix[j * tiles : (j + 1) * tiles] + offset), axis=0, keepdims=True
        )
        ranks.append(rank)
        offset = offset + jnp.sum(hits[j], axis=1, keepdims=True)
    tail = jnp.concatenate(
        [rows_ref[64:72, :].astype(F32), jnp.concatenate(misc, axis=1)], axis=0
    ).astype(BF16)
    payload = jnp.concatenate([rows_ref[0:64, :], tail], axis=0)
    rank = jnp.concatenate(ranks, axis=0).T
    target = jnp.concatenate(targets, axis=0).astype(F32).T
    slot = lax.broadcasted_iota(jnp.int32, (128, 128), 1).astype(F32).astype(BF16)
    one, zero = jnp.ones((), BF16), jnp.zeros((), BF16)
    spread = [
        [jnp.broadcast_to(x[:, j : j + 1], (128, 128)).astype(BF16) for j in range(chunks)]
        for x in (rank, target)
    ]
    hot = jnp.concatenate([jnp.where(x == slot, one, zero) for x in spread[0]], axis=0)
    target = jnp.concatenate(spread[1], axis=0)
    for pair in range(tiles // 2):
        chosen = [
            jnp.where(target == jnp.asarray(2.0 * pair + side, BF16), hot, zero)
            for side in range(2)
        ]
        packed = jnp.dot(
            payload, jnp.concatenate(chosen, axis=1), preferred_element_type=F32
        ).astype(BF16)
        out_ref[2 * pair] = packed[:, :128]
        out_ref[2 * pair + 1] = packed[:, 128:]


def add_column(total, x, source, target, width):
    lane = lanes_iota()
    here = (lane >= target) & (lane < target + width)
    return jnp.where(here, pltpu.roll(x, (target - source + 128) % 128, 1), total)


def prep_kernel(
    odd_ref,
    cells_ref,
    weights_ref,
    field_ref,
    u_ref,
    v_ref,
    k_ref,
    surface_ref,
    rows_one_ref,
    rows_two_ref,
    columns_one_ref,
    columns_two_ref,
):
    levels = k_ref.shape[0] // 8
    tracers = field_ref.shape[0] // (8 * levels)
    cell = rows_iota() * 128 + lanes_iota()
    surface = []
    for t in range(tracers):
        total = jnp.zeros((8, 128), F32)
        for s in range(cells_ref.shape[0]):
            total = total + jnp.where(cell == cells_ref[s], weights_ref[t, s], 0.0)
        surface.append(total)
        surface_ref[t] = total
    count = tracers * levels
    odd_row, odd_column = odd_ref[0] == 1, odd_ref[1] == 1

    def send(spot, values):
        rows_one_ref[spot, :] = jnp.where(odd_row, values[1], values[0])
        rows_two_ref[spot, :] = jnp.where(odd_row, values[0], values[1])

    send(slice(0, count), [field_ref[pl.ds(row, count, stride=8), :] for row in (7, 0)])
    for t in range(tracers):
        top = pl.ds(t * levels * 8, 8)
        total = field_ref[top, :] + surface[t]
        send(slice(t * levels, t * levels + 1), [total[row : row + 1, :] for row in (7, 0)])
    for i, plane in enumerate((u_ref, v_ref, k_ref)):
        at = count + i * levels
        send(slice(at, at + levels), [plane[pl.ds(row, levels, stride=8), :] for row in (7, 0)])

    def group(g, carry):
        east, west = list(carry[0]), list(carry[1])
        for j in range(GROUP):
            level = g * GROUP + j
            spot = pl.ds(level * 8, 8)
            values = [field_ref[pl.ds((t * levels + level) * 8, 8), :] for t in range(tracers)]
            if j == 0:
                values = [x + jnp.where(g == 0, add, 0.0) for x, add in zip(values, surface)]
            values += [u_ref[spot, :], v_ref[spot, :], k_ref[spot, :]]
            for i, x in enumerate(values):
                east[i] = add_column(east[i], x, 127, level, 1)
                west[i] = add_column(west[i], x, 0, level, 1)
        return tuple(east), tuple(west)

    zeros = (jnp.zeros((8, 128), F32),) * (tracers + 3)
    east, west = lax.fori_loop(0, levels // GROUP, group, (zeros, zeros))
    for i in range(tracers + 3):
        columns_one_ref[i] = jnp.where(odd_column, west[i], east[i])
        columns_two_ref[i] = jnp.where(odd_column, east[i], west[i])


def factor_kernel(k_ref, inverse_ref):
    def group(g, carry):
        below, inverse = carry
        for j in range(GROUP):
            spot = pl.ds((g * GROUP + j) * 8, 8)
            here = k_ref[spot, :]
            inverse = 1.0 / (1.0 + below + here - below * below * inverse)
            inverse_ref[spot, :] = inverse
            below = here
        return below, inverse

    zero = jnp.zeros((8, 128), F32)
    lax.fori_loop(0, k_ref.shape[0] // (8 * GROUP), group, (zero, zero))


class Advection:
    def __init__(self, u, v, inverse, below):
        self.lift = below * inverse
        self.east = jnp.maximum(u, 0.0) * inverse
        self.west = jnp.maximum(-u, 0.0) * inverse
        self.north = jnp.maximum(v, 0.0) * inverse
        self.south = jnp.maximum(-v, 0.0) * inverse
        self.centre = inverse - jnp.abs(u) * inverse - jnp.abs(v) * inverse

    def __call__(self, x, east, west, north, south):
        return (
            self.centre * x
            + self.east * east
            + self.west * west
            + self.north * north
            + self.south * south
        )


def shifted(x, east, west, north, south):
    lane, row = lanes_iota(), rows_iota()
    return (
        jnp.where(lane == 127, east, pltpu.roll(x, 127, 1)),
        jnp.where(lane == 0, west, pltpu.roll(x, 1, 1)),
        jnp.where(row == 7, north, pltpu.roll(x, 7, 0)),
        jnp.where(row == 0, south, pltpu.roll(x, 1, 0)),
    )


def first_kernel(
    odd_ref,
    field_ref,
    surface_ref,
    u_ref,
    v_ref,
    k_ref,
    inverse_ref,
    rows_one_ref,
    rows_two_ref,
    columns_one_ref,
    columns_two_ref,
    out_ref,
):
    levels = k_ref.shape[0] // 8
    tracers = field_ref.shape[0] // (8 * levels)
    zero = jnp.zeros((8, 128), F32)
    odd_row, odd_column = odd_ref[0] == 1, odd_ref[1] == 1
    both = [(columns_one_ref[t], columns_two_ref[t]) for t in range(tracers)]
    east = [jnp.where(odd_column, two, one) for one, two in both]
    west = [jnp.where(odd_column, one, two) for one, two in both]

    def forward(g, carry):
        below, state = carry[0], list(carry[1])
        for j in range(GROUP):
            level = g * GROUP + j
            spot = pl.ds(level * 8, 8)
            advect = Advection(u_ref[spot, :], v_ref[spot, :], inverse_ref[spot, :], below)
            for t in range(tracers):
                at = t * levels + level
                x = field_ref[pl.ds(at * 8, 8), :]
                if j == 0:
                    x = x + jnp.where(g == 0, surface_ref[t], 0.0)
                one, two = rows_one_ref[pl.ds(at, 1), :], rows_two_ref[pl.ds(at, 1), :]
                around = shifted(
                    x,
                    pltpu.roll(east[t], 127 - level, 1),
                    pltpu.roll(west[t], 128 - level, 1),
                    jnp.where(odd_row, two, one),
                    jnp.where(odd_row, one, two),
                )
                state[t] = advect(x, *around) + advect.lift * state[t]
                out_ref[pl.ds(at * 8, 8), :] = state[t]
            below = k_ref[spot, :]
        return below, tuple(state)

    lax.fori_loop(0, levels // GROUP, forward, (zero, (zero,) * tracers))
    back(levels, tracers, k_ref, inverse_ref, out_ref, ())


def back(levels, tracers, k_ref, inverse_ref, out_ref, others):
    zero = jnp.zeros((8, 128), F32)

    def group(g, state):
        state = list(state)
        for j in range(GROUP):
            level = levels - 1 - g * GROUP - j
            spot = pl.ds(level * 8, 8)
            upper = k_ref[spot, :] * inverse_ref[spot, :]
            for t in range(tracers):
                here = pl.ds((t * levels + level) * 8, 8)
                state[t] = out_ref[here, :] + upper * state[t]
                out_ref[here, :] = state[t]
            for i, (ref, k, inverse) in enumerate(others):
                i += tracers
                state[i] = ref[spot, :] + k[spot, :] * inverse[spot, :] * state[i]
                ref[spot, :] = state[i]
        return tuple(state)

    lax.fori_loop(0, levels // GROUP, group, (zero,) * (tracers + len(others)))


def ring_kernel(
    odd_ref,
    rows_one_ref,
    rows_two_ref,
    columns_one_ref,
    columns_two_ref,
    u_ref,
    v_ref,
    k_ref,
    inverse_ref,
    *column_refs,
):
    column_u_ref, column_v_ref, column_k_ref, column_inverse_ref = column_refs
    levels = u_ref.shape[0] // 8
    tracers = (rows_one_ref.shape[0] - 3 * levels) // levels
    above = rows_iota() < tracers
    from_one = above ^ (odd_ref[0] == 1)
    lane = lanes_iota()
    even = (lane & 1) == 0
    odd_column = odd_ref[1] == 1
    both = [(columns_one_ref[tracers + i], columns_two_ref[tracers + i]) for i in range(3)]
    east = [jnp.where(odd_column, two, one) for one, two in both]
    west = [jnp.where(odd_column, one, two) for one, two in both]
    zero = jnp.zeros((8, 128), F32)
    column_u_ref[...] = jnp.zeros_like(column_u_ref)
    column_v_ref[...] = jnp.zeros_like(column_v_ref)
    below, inverse, column_below, column_inverse = zero, zero, zero, zero
    for level in range(levels):
        spot = pl.ds(level * 8, 8)
        at = [tracers * levels + i * levels + level for i in range(3)]
        u, v, k = (
            jnp.where(from_one, rows_one_ref[pl.ds(i, 1), :], rows_two_ref[pl.ds(i, 1), :])
            for i in at
        )
        u_ref[spot, :] = u
        v_ref[spot, :] = jnp.where(above, v, -v)
        k_ref[spot, :] = k
        inverse = 1.0 / (1.0 + below + k - below * below * inverse)
        inverse_ref[spot, :] = inverse
        below = k
        u, v, k = (
            jnp.where(
                even,
                jnp.broadcast_to(e[:, level : level + 1], (8, 128)),
                jnp.broadcast_to(w[:, level : level + 1], (8, 128)),
            )
            for e, w in zip(east, west)
        )
        column_k_ref[spot, :] = k
        column_inverse = 1.0 / (1.0 + column_below + k - column_below * column_below * column_inverse)
        column_inverse_ref[spot, :] = column_inverse
        column_below = k
        packed = pl.ds(level // 16 * 8, 8)
        here = (lane >> 3) == level % 16
        column_u_ref[packed, :] = jnp.where(here, jnp.where(even, u, -u), column_u_ref[packed, :])
        column_v_ref[packed, :] = jnp.where(here, v, column_v_ref[packed, :])


def forcing_rows(received_ref, pairs):
    sources = received_ref.shape[0]
    levels, tracers = 72, 4
    count = tracers * levels
    rows = jnp.concatenate([received_ref[s, 0:levels, :] for s in range(sources)], axis=1)
    rows = rows.astype(F32)
    tail = jnp.concatenate([received_ref[s, 64:80, :] for s in range(sources)], axis=1).astype(F32)
    high, low = [], []
    for t in range(tracers):
        product = rows * tail[8 + t : 9 + t, :]
        high.append(product.astype(BF16))
        low.append((product - high[t].astype(F32)).astype(BF16))
    products = jnp.concatenate(high + low, axis=0)
    cell_row = tail[12:13, :]
    cell_lane = tail[13:14, :].astype(BF16)
    lane = lax.broadcasted_iota(jnp.int32, (128, sources * 128), 0).astype(F32).astype(BF16)
    hot = jnp.where(lane == cell_lane, jnp.ones((), BF16), jnp.zeros((), BF16))
    for pair in pairs:
        cells = jnp.concatenate(
            [hot * jnp.where(cell_row == r, 1.0, 0.0).astype(BF16) for r in pair], axis=0
        )
        both = lax.dot_general(
            products, cells, (((1,), (1,)), ((), ())), preferred_element_type=F32
        )
        yield both[:count] + both[count:]


EDGE_ROWS = ((0, 7), (1, 6))
INNER_ROWS = ((2, 3), (4, 5))


def edge_kernel(odd_ref, received_ref, first_ref, edge_ref, sent_one_ref, sent_two_ref):
    count = edge_ref.shape[1]
    levels = 72
    tracers = count // levels
    lane, row = lanes_iota(), rows_iota()
    zero = jnp.zeros((8, 128), F32)
    odd_row = odd_ref[0] == 1
    for at, (pair, both) in enumerate(zip(EDGE_ROWS, forcing_rows(received_ref, EDGE_ROWS))):
        down, up = (
            first_ref[pl.ds(r, count, stride=8), :] + both[:, i * 128 : (i + 1) * 128]
            for i, r in enumerate(pair)
        )
        edge_ref[2 * at] = down
        edge_ref[2 * at + 1] = up
        spot = slice(at * count, (at + 1) * count)
        sent_one_ref[spot, :] = jnp.where(odd_row, down, up)
        sent_two_ref[spot, :] = jnp.where(odd_row, up, down)
    for ref in (sent_one_ref, sent_two_ref):
        for at, source in ((2 * count, 126), (2 * count + 8, 0)):
            ref[at : at + 8, :] = zero
            for part in range((levels + 15) // 16):
                total = zero
                for start in range(16 * part, min(16 * part + 16, levels), 8):
                    for t in range(tracers):
                        x = ref[t * levels + start : t * levels + start + 8, :]
                        target = start % 16 * 8 + 2 * t
                        x = pltpu.roll(
                            x, (target - source + 128) % 128, 1, stride=8, stride_axis=0
                        )
                        total = jnp.where((lane - target - 8 * row) >> 1 == 0, x, total)
                ref[at + part : at + part + 1, :] = jnp.sum(total, axis=0, keepdims=True)


def inner_kernel(received_ref, first_ref, edge_ref, out_ref, east_ref, west_ref):
    count = edge_ref.shape[1]
    levels = 72
    tracers = count // levels
    for at, pair in enumerate(EDGE_ROWS):
        for i, r in enumerate(pair):
            out_ref[pl.ds(r, count, stride=8), :] = edge_ref[2 * at + i]
    for pair, both in zip(INNER_ROWS, forcing_rows(received_ref, INNER_ROWS)):
        for i, r in enumerate(pair):
            spot = pl.ds(r, count, stride=8)
            out_ref[spot, :] = first_ref[spot, :] + both[:, i * 128 : (i + 1) * 128]
    for part in range(east_ref.shape[0] // 8):
        east = jnp.zeros((8, 128), F32)
        west = jnp.zeros((8, 128), F32)
        for level in range(16 * part, min(16 * part + 16, levels)):
            for t in range(tracers):
                x = out_ref[pl.ds((t * levels + level) * 8, 8), :]
                target = level % 16 * 8 + 2 * t
                east = add_column(east, x, 126, target, 2)
                west = add_column(west, x, 0, target, 2)
        east_ref[part * 8 : part * 8 + 8, :] = east
        west_ref[part * 8 : part * 8 + 8, :] = west


def relay_kernel(odd_ref, one_ref, two_ref, east_ref, west_ref, sent_one_ref, sent_two_ref):
    rows = east_ref.shape[0]
    corner = one_ref.shape[0] - 16
    odd_row, odd_column = odd_ref[0] == 1, odd_ref[1] == 1

    def send(spot, values):
        sent_one_ref[spot, :] = jnp.where(odd_column, values[1], values[0])
        sent_two_ref[spot, :] = jnp.where(odd_column, values[0], values[1])

    send(slice(0, rows), [east_ref[...], west_ref[...]])
    ends = [[ref[at : at + 8, :] for at in (corner, corner + 8)] for ref in (one_ref, two_ref)]
    for at, side in ((rows, ~odd_row), (rows + 8, odd_row)):
        send(slice(at, at + 8), [jnp.where(side, one, two) for one, two in zip(*ends)])


def last_kernel(
    odd_ref,
    field_ref,
    u_ref,
    v_ref,
    k_ref,
    inverse_ref,
    rows_one_ref,
    rows_two_ref,
    columns_one_ref,
    columns_two_ref,
    own_west_ref,
    own_east_ref,
    ring_u_ref,
    ring_v_ref,
    ring_k_ref,
    ring_inverse_ref,
    column_u_ref,
    column_v_ref,
    column_k_ref,
    column_inverse_ref,
    out_ref,
    middle_ref,
    near_ref,
    far_ref,
    inner_ref,
    ring_ref,
    packed_ref,
    column_ref,
    sides_ref,
):
    levels = k_ref.shape[0] // 8
    tracers = field_ref.shape[0] // (8 * levels)
    count = tracers * levels
    parts = own_east_ref.shape[0] // 8
    lane, row = lanes_iota(), rows_iota()
    even = (lane & 1) == 0
    above = row < tracers
    zero = jnp.zeros((8, 128), F32)
    odd_row, odd_column = odd_ref[0] == 1, odd_ref[1] == 1
    sides_ref[0] = jnp.where(odd_column, columns_two_ref[...], columns_one_ref[...])
    sides_ref[1] = jnp.where(odd_column, columns_one_ref[...], columns_two_ref[...])
    for t in range(tracers):
        for side, (swap, edge) in enumerate(((odd_row, 7), (~odd_row, 0))):
            spot = pl.ds(side * tracers + t, levels, stride=8)
            at = t * levels
            for ref, start in ((near_ref, at), (far_ref, count + at)):
                rows = slice(start, start + levels)
                ref[spot, :] = jnp.where(swap, rows_two_ref[rows, :], rows_one_ref[rows, :])
            inner_ref[spot, :] = field_ref[pl.ds(at * 8 + edge, levels, stride=8), :]
    for part in range(parts):
        spot = pl.ds(part * 8, 8)
        east, west = sides_ref[0, spot, :], sides_ref[1, spot, :]
        x = jnp.where(even, east, west)
        outer = jnp.where(even, pltpu.roll(east, 127, 1), pltpu.roll(west, 1, 1))
        inner = jnp.where(
            even, pltpu.roll(own_east_ref[spot, :], 127, 1), pltpu.roll(own_west_ref[spot, :], 1, 1)
        )
        ends = [
            jnp.where(
                even,
                jnp.broadcast_to(sides_ref[0, pl.ds(at, 1), :], (8, 128)),
                jnp.broadcast_to(sides_ref[1, pl.ds(at, 1), :], (8, 128)),
            )
            for at in (parts * 8 + part, parts * 8 + 8 + part)
        ]
        north = jnp.where(row == 7, ends[0], pltpu.roll(x, 7, 0))
        south = jnp.where(row == 0, ends[1], pltpu.roll(x, 1, 0))
        advect = Advection(column_u_ref[spot, :], column_v_ref[spot, :], zero + 1.0, zero)
        packed_ref[spot, :] = advect(x, outer, inner, north, south)

    def forward(g, carry):
        below, ring_below, column_below = carry[0]
        state = list(carry[1])
        for j in range(GROUP):
            level = g * GROUP + j
            start = (level % 16) * 8
            part = level // 16
            packed = packed_ref[pl.ds(part * 8, 8), :]
            east = sides_ref[0, pl.ds(part * 8, 8), :]
            west = sides_ref[1, pl.ds(part * 8, 8), :]
            corner_east, corner_west = (
                jnp.where(
                    above,
                    jnp.broadcast_to(sides_ref[i, pl.ds(parts * 8 + part, 1), :], (8, 128)),
                    jnp.broadcast_to(sides_ref[i, pl.ds(parts * 8 + 8 + part, 1), :], (8, 128)),
                )
                for i in range(2)
            )
            spot = pl.ds(level * 8, 8)
            advect = Advection(u_ref[spot, :], v_ref[spot, :], inverse_ref[spot, :], below)
            for t in range(tracers):
                here = pl.ds((t * levels + level) * 8, 8)
                x = field_ref[here, :]
                around = shifted(
                    x,
                    pltpu.roll(east, 127 - start - 2 * t, 1),
                    pltpu.roll(west, 127 - start - 2 * t, 1),
                    near_ref[pl.ds(level * 8 + t, 1), :],
                    near_ref[pl.ds(level * 8 + tracers + t, 1), :],
                )
                state[t] = advect(x, *around) + advect.lift * state[t]
                middle_ref[here, :] = state[t]
            x = near_ref[spot, :]
            mine = start + 2 * (row % tracers)
            end_east = jnp.sum(jnp.where(lane == mine, corner_east, 0.0), axis=1, keepdims=True)
            end_west = jnp.sum(jnp.where(lane == mine + 1, corner_west, 0.0), axis=1, keepdims=True)
            advect = Advection(
                ring_u_ref[spot, :], ring_v_ref[spot, :], ring_inverse_ref[spot, :], ring_below
            )
            state[tracers] = (
                advect(
                    x,
                    jnp.where(lane == 127, end_east, pltpu.roll(x, 127, 1)),
                    jnp.where(lane == 0, end_west, pltpu.roll(x, 1, 1)),
                    far_ref[spot, :],
                    inner_ref[spot, :],
                )
                + advect.lift * state[tracers]
            )
            ring_ref[spot, :] = state[tracers]
            column_inverse = column_inverse_ref[spot, :]
            state[tracers + 1] = (
                pltpu.roll(packed, 128 - start, 1) * column_inverse
                + column_below * column_inverse * state[tracers + 1]
            )
            column_ref[spot, :] = state[tracers + 1]
            below, ring_below, column_below = (
                k_ref[spot, :],
                ring_k_ref[spot, :],
                column_k_ref[spot, :],
            )
        return (below, ring_below, column_below), tuple(state)

    lax.fori_loop(
        0, levels // GROUP, forward, ((zero, zero, zero), (zero,) * (tracers + 2))
    )
    back(
        levels,
        tracers,
        k_ref,
        inverse_ref,
        middle_ref,
        (
            (ring_ref, ring_k_ref, ring_inverse_ref),
            (column_ref, column_k_ref, column_inverse_ref),
        ),
    )

    def final(g, carry):
        below, state = carry[0], list(carry[1])
        for j in range(GROUP):
            level = g * GROUP + j
            spot = pl.ds(level * 8, 8)
            advect = Advection(u_ref[spot, :], v_ref[spot, :], inverse_ref[spot, :], below)
            sides = column_ref[spot, :]
            for t in range(tracers):
                here = pl.ds((t * levels + level) * 8, 8)
                x = middle_ref[here, :]
                around = shifted(
                    x,
                    pltpu.roll(sides, 127 - 2 * t, 1),
                    pltpu.roll(sides, 127 - 2 * t, 1),
                    ring_ref[pl.ds(level * 8 + t, 1), :],
                    ring_ref[pl.ds(level * 8 + tracers + t, 1), :],
                )
                state[t] = advect(x, *around) + advect.lift * state[t]
                out_ref[here, :] = state[t]
            below = k_ref[spot, :]
        return below, tuple(state)

    lax.fori_loop(0, levels // GROUP, final, (zero, (zero,) * tracers))
    back(levels, tracers, k_ref, inverse_ref, out_ref, ())


def swap(one, two, axis, periodic):
    size = lax.axis_size(axis)
    pairs = [(i, (i + 1) % size) for i in range(size if periodic else size - 1)]
    both = [[(a, b) for p in pairs[start::2] for a, b in (p, p[::-1])] for start in (0, 1)]
    return lax.ppermute(one, axis, both[0]), lax.ppermute(two, axis, both[1])


def body(
    adjoint_in,
    wind_u,
    wind_v,
    diffusion,
    kernel_rows,
    retrieval_misfit,
    retrieval_columns,
    retrieval_counts,
    station_cells,
    station_misfit,
):
    tracers, levels, lat_rows, lon_cells = adjoint_in.shape
    slots = kernel_rows.shape[1]
    tiles = lax.axis_size("lon")
    parts = (levels + 15) // 16
    full = jax.ShapeDtypeStruct((tracers * levels * 8, 128), F32)
    planes = jax.ShapeDtypeStruct((levels * 8, 128), F32)
    rows_one = jax.ShapeDtypeStruct(((tracers + 3) * levels, 128), F32)
    columns_one = jax.ShapeDtypeStruct((tracers + 3, 8, 128), F32)
    rows_two = jax.ShapeDtypeStruct((2 * tracers * levels + 16, 128), F32)
    columns_two = jax.ShapeDtypeStruct((parts * 8, 128), F32)
    columns_sent = jax.ShapeDtypeStruct((parts * 8 + 16, 128), F32)

    packed = pl.pallas_call(
        pack_kernel,
        out_shape=jax.ShapeDtypeStruct((tiles, 80, 128), BF16),
        in_specs=[pl.BlockSpec(memory_space=pltpu.SMEM)]
        + [pl.BlockSpec(memory_space=pltpu.VMEM)] * 3,
        compiler_params=pltpu.CompilerParams(vmem_limit_bytes=56 << 20),
        name="pack",
    )(retrieval_counts, kernel_rows, retrieval_misfit, retrieval_columns.reshape(slots // 128, 128))
    received = lax.all_to_all(packed, "lon", split_axis=0, concat_axis=0, tiled=True)

    field = adjoint_in.reshape(full.shape)
    u = wind_u.reshape(planes.shape)
    v = wind_v.reshape(planes.shape)
    k = diffusion.reshape(planes.shape)
    odd = jnp.stack([lax.axis_index("lat") & 1, lax.axis_index("lon") & 1])
    surface, *sent = vmem_call(
        prep_kernel,
        out_shape=(
            jax.ShapeDtypeStruct((tracers, 8, 128), F32),
            rows_one,
            rows_one,
            columns_one,
            columns_one,
        ),
        smem=3,
        name="prep",
    )(odd, station_cells, station_misfit, field, u, v, k)
    edges = swap(*sent[:2], "lat", False) + swap(*sent[2:], "lon", True)
    inverse = vmem_call(factor_kernel, out_shape=planes, name="factor")(k)
    ring = vmem_call(
        ring_kernel,
        out_shape=(planes,) * 4 + (columns_two,) * 2 + (planes,) * 2,
        smem=1,
        name="ring",
    )(odd, *edges)
    first = vmem_call(first_kernel, out_shape=full, smem=1, name="first")(
        odd, field, surface, u, v, k, inverse, *edges
    )
    edge, *sent = vmem_call(
        edge_kernel,
        out_shape=(
            jax.ShapeDtypeStruct((4, tracers * levels, 128), F32),
            rows_two,
            rows_two,
        ),
        smem=1,
        limit=30,
        name="edge",
    )(odd, received, first)
    injected, east, west = vmem_call(
        inner_kernel, out_shape=(full, columns_two, columns_two), limit=30, name="inner"
    )(received, first, edge)
    rows = swap(*sent, "lat", False)
    sent = vmem_call(relay_kernel, out_shape=(columns_sent,) * 2, smem=1, name="relay")(
        odd, *rows, east, west
    )
    columns = swap(*sent, "lon", True)
    last = vmem_call(
        last_kernel,
        out_shape=full,
        smem=1,
        scratch=(full,)
        + (planes,) * 4
        + (columns_two, planes, jax.ShapeDtypeStruct((2,) + columns_sent.shape, F32)),
        name="last",
    )(odd, injected, u, v, k, inverse, *rows, *columns, west, east, *ring)
    return last.reshape(adjoint_in.shape)


def solution(mesh):
    return jax.shard_map(
        body,
        mesh=mesh,
        in_specs=(
            P(None, None, "lat", "lon"),
            P(None, "lat", "lon"),
            P(None, "lat", "lon"),
            P(None, "lat", "lon"),
            P(None, ("lat", "lon")),
            P(None, ("lat", "lon")),
            P(("lat", "lon")),
            P(("lat", "lon")),
            P(("lat", "lon")),
            P(None, ("lat", "lon")),
        ),
        out_specs=P(None, None, "lat", "lon"),
        check_vma=False,
    )
```

```python
import jax
import jax.numpy as jnp
from jax import lax
from jax.experimental import pallas as pl
from jax.experimental.pallas import tpu as pltpu
from jax.sharding import PartitionSpec as P

F32 = jnp.float32
BF16 = jnp.bfloat16
GROUP = 72


def vmem_call(kernel, *, out_shape, smem=0, scratch=(), copies=0, limit=16, name):
    is_tuple = isinstance(out_shape, tuple)
    outs = out_shape if is_tuple else (out_shape,)
    outs = tuple(pltpu.VMEM(o.shape, o.dtype) for o in outs)

    def run(*args):
        args = args[:smem] + tuple(
            pltpu.with_memory_space_constraint(a, pltpu.VMEM) for a in args[smem:]
        )
        specs = [pl.BlockSpec(memory_space=pltpu.SMEM)] * smem
        specs += [pl.BlockSpec(memory_space=pltpu.VMEM)] * (len(args) - smem)
        own = {"out_specs": pl.BlockSpec(memory_space=pl.ANY)} if copies else {}
        return pl.pallas_call(
            kernel,
            out_shape=out_shape if copies else outs if is_tuple else outs[0],
            in_specs=specs,
            scratch_shapes=[pltpu.VMEM(o.shape, o.dtype) for o in scratch]
            + [pltpu.SemaphoreType.DMA((copies,))] * (copies > 0),
            **own,
            compiler_params=pltpu.CompilerParams(vmem_limit_bytes=limit << 20),
            name=name,
        )(*args)

    return run


def lanes_iota():
    return lax.broadcasted_iota(jnp.int32, (8, 128), 1)


def rows_iota():
    return lax.broadcasted_iota(jnp.int32, (8, 128), 0)


def pack_kernel(count_ref, rows_ref, misfit_ref, columns_ref, out_ref):
    chunks = columns_ref.shape[0]
    tiles = out_ref.shape[0]
    count = count_ref[...]
    lane = lax.broadcasted_iota(jnp.int32, (1, 128), 1)
    tile = lax.broadcasted_iota(jnp.int32, (tiles, 128), 0)
    hits = []
    targets = []
    misc = []
    for j in range(chunks):
        column = columns_ref[j : j + 1, :]
        live = (lane + j * 128) < count
        target = jnp.where(live, column >> 10, -1)
        targets.append(target)
        hits.append((tile == target).astype(F32))
        cell = column & 1023
        misc.append(
            jnp.concatenate(
                [
                    misfit_ref[:, j * 128 : (j + 1) * 128].astype(F32),
                    (cell >> 7).astype(F32),
                    (cell & 127).astype(F32),
                    jnp.zeros((2, 128), F32),
                ],
                axis=0,
            )
        )
    before = lax.broadcasted_iota(jnp.int32, (128, 128), 0) < lax.broadcasted_iota(
        jnp.int32, (128, 128), 1
    )
    prefix = jnp.dot(
        jnp.concatenate(hits, axis=0).astype(BF16),
        before.astype(F32).astype(BF16),
        preferred_element_type=F32,
    )
    offset = jnp.zeros((tiles, 1), F32)
    ranks = []
    for j in range(chunks):
        rank = jnp.sum(
            hits[j] * (prefix[j * tiles : (j + 1) * tiles] + offset), axis=0, keepdims=True
        )
        ranks.append(rank)
        offset = offset + jnp.sum(hits[j], axis=1, keepdims=True)
    tail = jnp.concatenate(
        [rows_ref[64:72, :].astype(F32), jnp.concatenate(misc, axis=1)], axis=0
    ).astype(BF16)
    payload = jnp.concatenate([rows_ref[0:64, :], tail], axis=0)
    rank = jnp.concatenate(ranks, axis=0).T
    target = jnp.concatenate(targets, axis=0).astype(F32).T
    slot = lax.broadcasted_iota(jnp.int32, (128, 128), 1).astype(F32).astype(BF16)
    one, zero = jnp.ones((), BF16), jnp.zeros((), BF16)
    spread = [
        [jnp.broadcast_to(x[:, j : j + 1], (128, 128)).astype(BF16) for j in range(chunks)]
        for x in (rank, target)
    ]
    hot = jnp.concatenate([jnp.where(x == slot, one, zero) for x in spread[0]], axis=0)
    target = jnp.concatenate(spread[1], axis=0)
    for pair in range(tiles // 2):
        chosen = [
            jnp.where(target == jnp.asarray(2.0 * pair + side, BF16), hot, zero)
            for side in range(2)
        ]
        packed = jnp.dot(
            payload, jnp.concatenate(chosen, axis=1), preferred_element_type=F32
        ).astype(BF16)
        out_ref[2 * pair] = packed[:, :128]
        out_ref[2 * pair + 1] = packed[:, 128:]


def add_column(total, x, source, target, width):
    lane = lanes_iota()
    here = (lane >= target) & (lane < target + width)
    return jnp.where(here, pltpu.roll(x, (target - source + 128) % 128, 1), total)


def prep_kernel(
    odd_ref,
    cells_ref,
    weights_ref,
    field_ref,
    u_ref,
    v_ref,
    k_ref,
    surface_ref,
    rows_one_ref,
    rows_two_ref,
    columns_one_ref,
    columns_two_ref,
):
    levels = k_ref.shape[0] // 8
    tracers = field_ref.shape[0] // (8 * levels)
    cell = rows_iota() * 128 + lanes_iota()
    surface = []
    for t in range(tracers):
        total = jnp.zeros((8, 128), F32)
        for s in range(cells_ref.shape[0]):
            total = total + jnp.where(cell == cells_ref[s], weights_ref[t, s], 0.0)
        surface.append(total)
        surface_ref[t] = total
    count = tracers * levels
    odd_row, odd_column = odd_ref[0] == 1, odd_ref[1] == 1

    def send(spot, values):
        rows_one_ref[spot, :] = jnp.where(odd_row, values[1], values[0])
        rows_two_ref[spot, :] = jnp.where(odd_row, values[0], values[1])

    send(slice(0, count), [field_ref[pl.ds(row, count, stride=8), :] for row in (7, 0)])
    for t in range(tracers):
        top = pl.ds(t * levels * 8, 8)
        total = field_ref[top, :] + surface[t]
        send(slice(t * levels, t * levels + 1), [total[row : row + 1, :] for row in (7, 0)])
    for i, plane in enumerate((u_ref, v_ref, k_ref)):
        at = count + i * levels
        send(slice(at, at + levels), [plane[pl.ds(row, levels, stride=8), :] for row in (7, 0)])

    def group(g, carry):
        east, west = list(carry[0]), list(carry[1])
        for j in range(GROUP):
            level = g * GROUP + j
            spot = pl.ds(level * 8, 8)
            values = [field_ref[pl.ds((t * levels + level) * 8, 8), :] for t in range(tracers)]
            if j == 0:
                values = [x + jnp.where(g == 0, add, 0.0) for x, add in zip(values, surface)]
            values += [u_ref[spot, :], v_ref[spot, :], k_ref[spot, :]]
            for i, x in enumerate(values):
                east[i] = add_column(east[i], x, 127, level, 1)
                west[i] = add_column(west[i], x, 0, level, 1)
        return tuple(east), tuple(west)

    zeros = (jnp.zeros((8, 128), F32),) * (tracers + 3)
    east, west = lax.fori_loop(0, levels // GROUP, group, (zeros, zeros))
    for i in range(tracers + 3):
        columns_one_ref[i] = jnp.where(odd_column, west[i], east[i])
        columns_two_ref[i] = jnp.where(odd_column, east[i], west[i])


def factor_kernel(k_ref, inverse_ref):
    def group(g, carry):
        below, inverse = carry
        for j in range(GROUP):
            spot = pl.ds((g * GROUP + j) * 8, 8)
            here = k_ref[spot, :]
            inverse = 1.0 / (1.0 + below + here - below * below * inverse)
            inverse_ref[spot, :] = inverse
            below = here
        return below, inverse

    zero = jnp.zeros((8, 128), F32)
    lax.fori_loop(0, k_ref.shape[0] // (8 * GROUP), group, (zero, zero))


class Advection:
    def __init__(self, u, v, inverse, below):
        self.lift = below * inverse
        self.east = jnp.maximum(u, 0.0) * inverse
        self.west = jnp.maximum(-u, 0.0) * inverse
        self.north = jnp.maximum(v, 0.0) * inverse
        self.south = jnp.maximum(-v, 0.0) * inverse
        self.centre = inverse - jnp.abs(u) * inverse - jnp.abs(v) * inverse

    def __call__(self, x, east, west, north, south):
        return (
            self.centre * x
            + self.east * east
            + self.west * west
            + self.north * north
            + self.south * south
        )


def shifted(x, east, west, north, south):
    lane, row = lanes_iota(), rows_iota()
    return (
        jnp.where(lane == 127, east, pltpu.roll(x, 127, 1)),
        jnp.where(lane == 0, west, pltpu.roll(x, 1, 1)),
        jnp.where(row == 7, north, pltpu.roll(x, 7, 0)),
        jnp.where(row == 0, south, pltpu.roll(x, 1, 0)),
    )


def first_kernel(
    odd_ref,
    field_ref,
    surface_ref,
    u_ref,
    v_ref,
    k_ref,
    inverse_ref,
    rows_one_ref,
    rows_two_ref,
    columns_one_ref,
    columns_two_ref,
    out_ref,
):
    levels = k_ref.shape[0] // 8
    tracers = field_ref.shape[0] // (8 * levels)
    zero = jnp.zeros((8, 128), F32)
    odd_row, odd_column = odd_ref[0] == 1, odd_ref[1] == 1
    both = [(columns_one_ref[t], columns_two_ref[t]) for t in range(tracers)]
    east = [jnp.where(odd_column, two, one) for one, two in both]
    west = [jnp.where(odd_column, one, two) for one, two in both]

    def forward(g, carry):
        below, state = carry[0], list(carry[1])
        for j in range(GROUP):
            level = g * GROUP + j
            spot = pl.ds(level * 8, 8)
            advect = Advection(u_ref[spot, :], v_ref[spot, :], inverse_ref[spot, :], below)
            for t in range(tracers):
                at = t * levels + level
                x = field_ref[pl.ds(at * 8, 8), :]
                if j == 0:
                    x = x + jnp.where(g == 0, surface_ref[t], 0.0)
                one, two = rows_one_ref[pl.ds(at, 1), :], rows_two_ref[pl.ds(at, 1), :]
                around = shifted(
                    x,
                    pltpu.roll(east[t], 127 - level, 1),
                    pltpu.roll(west[t], 128 - level, 1),
                    jnp.where(odd_row, two, one),
                    jnp.where(odd_row, one, two),
                )
                state[t] = advect(x, *around) + advect.lift * state[t]
                out_ref[pl.ds(at * 8, 8), :] = state[t]
            below = k_ref[spot, :]
        return below, tuple(state)

    lax.fori_loop(0, levels // GROUP, forward, (zero, (zero,) * tracers))
    back(levels, tracers, k_ref, inverse_ref, out_ref, ())


def back(levels, tracers, k_ref, inverse_ref, out_ref, others):
    zero = jnp.zeros((8, 128), F32)

    def group(g, state):
        state = list(state)
        for j in range(GROUP):
            level = levels - 1 - g * GROUP - j
            spot = pl.ds(level * 8, 8)
            upper = k_ref[spot, :] * inverse_ref[spot, :]
            for t in range(tracers):
                here = pl.ds((t * levels + level) * 8, 8)
                state[t] = out_ref[here, :] + upper * state[t]
                out_ref[here, :] = state[t]
            for i, (ref, k, inverse) in enumerate(others):
                i += tracers
                state[i] = ref[spot, :] + k[spot, :] * inverse[spot, :] * state[i]
                ref[spot, :] = state[i]
        return tuple(state)

    lax.fori_loop(0, levels // GROUP, group, (zero,) * (tracers + len(others)))


def ring_kernel(
    odd_ref,
    rows_one_ref,
    rows_two_ref,
    columns_one_ref,
    columns_two_ref,
    u_ref,
    v_ref,
    k_ref,
    inverse_ref,
    *column_refs,
):
    column_u_ref, column_v_ref, column_k_ref, column_inverse_ref = column_refs
    levels = u_ref.shape[0] // 8
    tracers = (rows_one_ref.shape[0] - 3 * levels) // levels
    above = rows_iota() < tracers
    from_one = above ^ (odd_ref[0] == 1)
    lane = lanes_iota()
    even = (lane & 1) == 0
    odd_column = odd_ref[1] == 1
    both = [(columns_one_ref[tracers + i], columns_two_ref[tracers + i]) for i in range(3)]
    east = [jnp.where(odd_column, two, one) for one, two in both]
    west = [jnp.where(odd_column, one, two) for one, two in both]
    zero = jnp.zeros((8, 128), F32)
    column_u_ref[...] = jnp.zeros_like(column_u_ref)
    column_v_ref[...] = jnp.zeros_like(column_v_ref)
    below, inverse, column_below, column_inverse = zero, zero, zero, zero
    for level in range(levels):
        spot = pl.ds(level * 8, 8)
        at = [tracers * levels + i * levels + level for i in range(3)]
        u, v, k = (
            jnp.where(from_one, rows_one_ref[pl.ds(i, 1), :], rows_two_ref[pl.ds(i, 1), :])
            for i in at
        )
        u_ref[spot, :] = u
        v_ref[spot, :] = jnp.where(above, v, -v)
        k_ref[spot, :] = k
        inverse = 1.0 / (1.0 + below + k - below * below * inverse)
        inverse_ref[spot, :] = inverse
        below = k
        u, v, k = (
            jnp.where(
                even,
                jnp.broadcast_to(e[:, level : level + 1], (8, 128)),
                jnp.broadcast_to(w[:, level : level + 1], (8, 128)),
            )
            for e, w in zip(east, west)
        )
        column_k_ref[spot, :] = k
        column_inverse = 1.0 / (1.0 + column_below + k - column_below * column_below * column_inverse)
        column_inverse_ref[spot, :] = column_inverse
        column_below = k
        packed = pl.ds(level // 16 * 8, 8)
        here = (lane >> 3) == level % 16
        column_u_ref[packed, :] = jnp.where(here, jnp.where(even, u, -u), column_u_ref[packed, :])
        column_v_ref[packed, :] = jnp.where(here, v, column_v_ref[packed, :])


def forcing_rows(received_ref, pairs):
    sources = received_ref.shape[0]
    levels, tracers = 72, 4
    count = tracers * levels
    rows = jnp.concatenate([received_ref[s, 0:levels, :] for s in range(sources)], axis=1)
    rows = rows.astype(F32)
    tail = jnp.concatenate([received_ref[s, 64:80, :] for s in range(sources)], axis=1).astype(F32)
    high, low = [], []
    for t in range(tracers):
        product = rows * tail[8 + t : 9 + t, :]
        high.append(product.astype(BF16))
        low.append((product - high[t].astype(F32)).astype(BF16))
    products = jnp.concatenate(high + low, axis=0)
    cell_row = tail[12:13, :]
    cell_lane = tail[13:14, :].astype(BF16)
    lane = lax.broadcasted_iota(jnp.int32, (128, sources * 128), 0).astype(F32).astype(BF16)
    hot = jnp.where(lane == cell_lane, jnp.ones((), BF16), jnp.zeros((), BF16))
    for pair in pairs:
        cells = jnp.concatenate(
            [hot * jnp.where(cell_row == r, 1.0, 0.0).astype(BF16) for r in pair], axis=0
        )
        both = lax.dot_general(
            products, cells, (((1,), (1,)), ((), ())), preferred_element_type=F32
        )
        yield both[:count] + both[count:]


EDGE_ROWS = ((0, 7), (1, 6))
INNER_ROWS = ((2, 3), (4, 5))


def edge_kernel(odd_ref, received_ref, first_ref, *refs):
    edge_ref, sent_one_ref, sent_two_ref = refs[-3:]
    count = edge_ref.shape[1]
    levels = 72
    tracers = count // levels
    lane, row = lanes_iota(), rows_iota()
    zero = jnp.zeros((8, 128), F32)
    odd_row = odd_ref[0] == 1
    for at, (pair, both) in enumerate(zip(EDGE_ROWS, forcing_rows(received_ref, EDGE_ROWS))):
        down, up = (
            first_ref[pl.ds(r, count, stride=8), :] + both[:, i * 128 : (i + 1) * 128]
            for i, r in enumerate(pair)
        )
        edge_ref[2 * at] = down
        edge_ref[2 * at + 1] = up
        spot = slice(at * count, (at + 1) * count)
        sent_one_ref[spot, :] = jnp.where(odd_row, down, up)
        sent_two_ref[spot, :] = jnp.where(odd_row, up, down)
    for ref in (sent_one_ref, sent_two_ref):
        for at, source in ((2 * count, 126), (2 * count + 8, 0)):
            ref[at : at + 8, :] = zero
            for part in range((levels + 15) // 16):
                total = zero
                for start in range(16 * part, min(16 * part + 16, levels), 8):
                    for t in range(tracers):
                        x = ref[t * levels + start : t * levels + start + 8, :]
                        target = start % 16 * 8 + 2 * t
                        x = pltpu.roll(
                            x, (target - source + 128) % 128, 1, stride=8, stride_axis=0
                        )
                        total = jnp.where((lane - target - 8 * row) >> 1 == 0, x, total)
                ref[at + part : at + part + 1, :] = jnp.sum(total, axis=0, keepdims=True)


def inner_kernel(received_ref, first_ref, edge_ref, *refs):
    out_ref, east_ref, west_ref = refs[-3:]
    count = edge_ref.shape[1]
    levels = 72
    tracers = count // levels
    for at, pair in enumerate(EDGE_ROWS):
        for i, r in enumerate(pair):
            out_ref[pl.ds(r, count, stride=8), :] = edge_ref[2 * at + i]
    for pair, both in zip(INNER_ROWS, forcing_rows(received_ref, INNER_ROWS)):
        for i, r in enumerate(pair):
            spot = pl.ds(r, count, stride=8)
            out_ref[spot, :] = first_ref[spot, :] + both[:, i * 128 : (i + 1) * 128]
    for part in range(east_ref.shape[0] // 8):
        east = jnp.zeros((8, 128), F32)
        west = jnp.zeros((8, 128), F32)
        for level in range(16 * part, min(16 * part + 16, levels)):
            for t in range(tracers):
                x = out_ref[pl.ds((t * levels + level) * 8, 8), :]
                target = level % 16 * 8 + 2 * t
                east = add_column(east, x, 126, target, 2)
                west = add_column(west, x, 0, target, 2)
        east_ref[part * 8 : part * 8 + 8, :] = east
        west_ref[part * 8 : part * 8 + 8, :] = west


def relay_kernel(odd_ref, one_ref, two_ref, east_ref, west_ref, sent_one_ref, sent_two_ref):
    rows = east_ref.shape[0]
    corner = one_ref.shape[0] - 16
    odd_row, odd_column = odd_ref[0] == 1, odd_ref[1] == 1

    def send(spot, values):
        sent_one_ref[spot, :] = jnp.where(odd_column, values[1], values[0])
        sent_two_ref[spot, :] = jnp.where(odd_column, values[0], values[1])

    send(slice(0, rows), [east_ref[...], west_ref[...]])
    ends = [[ref[at : at + 8, :] for at in (corner, corner + 8)] for ref in (one_ref, two_ref)]
    for at, side in ((rows, ~odd_row), (rows + 8, odd_row)):
        send(slice(at, at + 8), [jnp.where(side, one, two) for one, two in zip(*ends)])


def last_kernel(
    odd_ref,
    field_ref,
    u_ref,
    v_ref,
    k_ref,
    inverse_ref,
    rows_one_ref,
    rows_two_ref,
    columns_one_ref,
    columns_two_ref,
    own_west_ref,
    own_east_ref,
    ring_u_ref,
    ring_v_ref,
    ring_k_ref,
    ring_inverse_ref,
    column_u_ref,
    column_v_ref,
    column_k_ref,
    column_inverse_ref,
    result_ref,
    middle_ref,
    near_ref,
    far_ref,
    inner_ref,
    ring_ref,
    packed_ref,
    column_ref,
    sides_ref,
    out_ref,
    copied_ref,
):
    levels = k_ref.shape[0] // 8
    tracers = field_ref.shape[0] // (8 * levels)
    count = tracers * levels
    parts = own_east_ref.shape[0] // 8
    lane, row = lanes_iota(), rows_iota()
    even = (lane & 1) == 0
    above = row < tracers
    zero = jnp.zeros((8, 128), F32)
    odd_row, odd_column = odd_ref[0] == 1, odd_ref[1] == 1
    sides_ref[0] = jnp.where(odd_column, columns_two_ref[...], columns_one_ref[...])
    sides_ref[1] = jnp.where(odd_column, columns_one_ref[...], columns_two_ref[...])
    for t in range(tracers):
        for side, (swap, edge) in enumerate(((odd_row, 7), (~odd_row, 0))):
            spot = pl.ds(side * tracers + t, levels, stride=8)
            at = t * levels
            for ref, start in ((near_ref, at), (far_ref, count + at)):
                rows = slice(start, start + levels)
                ref[spot, :] = jnp.where(swap, rows_two_ref[rows, :], rows_one_ref[rows, :])
            inner_ref[spot, :] = field_ref[pl.ds(at * 8 + edge, levels, stride=8), :]
    for part in range(parts):
        spot = pl.ds(part * 8, 8)
        east, west = sides_ref[0, spot, :], sides_ref[1, spot, :]
        x = jnp.where(even, east, west)
        outer = jnp.where(even, pltpu.roll(east, 127, 1), pltpu.roll(west, 1, 1))
        inner = jnp.where(
            even, pltpu.roll(own_east_ref[spot, :], 127, 1), pltpu.roll(own_west_ref[spot, :], 1, 1)
        )
        ends = [
            jnp.where(
                even,
                jnp.broadcast_to(sides_ref[0, pl.ds(at, 1), :], (8, 128)),
                jnp.broadcast_to(sides_ref[1, pl.ds(at, 1), :], (8, 128)),
            )
            for at in (parts * 8 + part, parts * 8 + 8 + part)
        ]
        north = jnp.where(row == 7, ends[0], pltpu.roll(x, 7, 0))
        south = jnp.where(row == 0, ends[1], pltpu.roll(x, 1, 0))
        advect = Advection(column_u_ref[spot, :], column_v_ref[spot, :], zero + 1.0, zero)
        packed_ref[spot, :] = advect(x, outer, inner, north, south)

    def forward(g, carry):
        below, ring_below, column_below = carry[0]
        state = list(carry[1])
        for j in range(GROUP):
            level = g * GROUP + j
            start = (level % 16) * 8
            part = level // 16
            packed = packed_ref[pl.ds(part * 8, 8), :]
            east = sides_ref[0, pl.ds(part * 8, 8), :]
            west = sides_ref[1, pl.ds(part * 8, 8), :]
            corner_east, corner_west = (
                jnp.where(
                    above,
                    jnp.broadcast_to(sides_ref[i, pl.ds(parts * 8 + part, 1), :], (8, 128)),
                    jnp.broadcast_to(sides_ref[i, pl.ds(parts * 8 + 8 + part, 1), :], (8, 128)),
                )
                for i in range(2)
            )
            spot = pl.ds(level * 8, 8)
            advect = Advection(u_ref[spot, :], v_ref[spot, :], inverse_ref[spot, :], below)
            for t in range(tracers):
                here = pl.ds((t * levels + level) * 8, 8)
                x = field_ref[here, :]
                around = shifted(
                    x,
                    pltpu.roll(east, 127 - start - 2 * t, 1),
                    pltpu.roll(west, 127 - start - 2 * t, 1),
                    near_ref[pl.ds(level * 8 + t, 1), :],
                    near_ref[pl.ds(level * 8 + tracers + t, 1), :],
                )
                state[t] = advect(x, *around) + advect.lift * state[t]
                middle_ref[here, :] = state[t]
            x = near_ref[spot, :]
            mine = start + 2 * (row % tracers)
            end_east = jnp.sum(jnp.where(lane == mine, corner_east, 0.0), axis=1, keepdims=True)
            end_west = jnp.sum(jnp.where(lane == mine + 1, corner_west, 0.0), axis=1, keepdims=True)
            advect = Advection(
                ring_u_ref[spot, :], ring_v_ref[spot, :], ring_inverse_ref[spot, :], ring_below
            )
            state[tracers] = (
                advect(
                    x,
                    jnp.where(lane == 127, end_east, pltpu.roll(x, 127, 1)),
                    jnp.where(lane == 0, end_west, pltpu.roll(x, 1, 1)),
                    far_ref[spot, :],
                    inner_ref[spot, :],
                )
                + advect.lift * state[tracers]
            )
            ring_ref[spot, :] = state[tracers]
            column_inverse = column_inverse_ref[spot, :]
            state[tracers + 1] = (
                pltpu.roll(packed, 128 - start, 1) * column_inverse
                + column_below * column_inverse * state[tracers + 1]
            )
            column_ref[spot, :] = state[tracers + 1]
            below, ring_below, column_below = (
                k_ref[spot, :],
                ring_k_ref[spot, :],
                column_k_ref[spot, :],
            )
        return (below, ring_below, column_below), tuple(state)

    lax.fori_loop(
        0, levels // GROUP, forward, ((zero, zero, zero), (zero,) * (tracers + 2))
    )
    back(
        levels,
        tracers,
        k_ref,
        inverse_ref,
        middle_ref,
        (
            (ring_ref, ring_k_ref, ring_inverse_ref),
            (column_ref, column_k_ref, column_inverse_ref),
        ),
    )

    def final(g, carry):
        below, state = carry[0], list(carry[1])
        for j in range(GROUP):
            level = g * GROUP + j
            spot = pl.ds(level * 8, 8)
            advect = Advection(u_ref[spot, :], v_ref[spot, :], inverse_ref[spot, :], below)
            sides = column_ref[spot, :]
            for t in range(tracers):
                here = pl.ds((t * levels + level) * 8, 8)
                x = middle_ref[here, :]
                around = shifted(
                    x,
                    pltpu.roll(sides, 127 - 2 * t, 1),
                    pltpu.roll(sides, 127 - 2 * t, 1),
                    ring_ref[pl.ds(level * 8 + t, 1), :],
                    ring_ref[pl.ds(level * 8 + tracers + t, 1), :],
                )
                state[t] = advect(x, *around) + advect.lift * state[t]
                out_ref[here, :] = state[t]
            below = k_ref[spot, :]
        return below, tuple(state)

    lax.fori_loop(0, levels // GROUP, final, (zero, (zero,) * tracers))

    state = [zero] * tracers
    size = levels // (copied_ref.shape[0] // tracers)
    copies = []
    for level in range(levels - 1, -1, -1):
        spot = pl.ds(level * 8, 8)
        upper = k_ref[spot, :] * inverse_ref[spot, :]
        for t in range(tracers):
            here = pl.ds((t * levels + level) * 8, 8)
            state[t] = out_ref[here, :] + upper * state[t]
            out_ref[here, :] = state[t]
        if level % size == 0:
            for t in range(tracers):
                part = pl.ds((t * levels + level) * 8, size * 8)
                copies.append(
                    pltpu.make_async_copy(
                        out_ref.at[part, :], result_ref.at[part, :], copied_ref.at[len(copies)]
                    )
                )
                copies[-1].start()
    for copy in copies:
        copy.wait()


def swap(one, two, axis, periodic):
    size = lax.axis_size(axis)
    pairs = [(i, (i + 1) % size) for i in range(size if periodic else size - 1)]
    both = [[(a, b) for p in pairs[start::2] for a, b in (p, p[::-1])] for start in (0, 1)]
    return lax.ppermute(one, axis, both[0]), lax.ppermute(two, axis, both[1])


def body(
    adjoint_in,
    wind_u,
    wind_v,
    diffusion,
    kernel_rows,
    retrieval_misfit,
    retrieval_columns,
    retrieval_counts,
    station_cells,
    station_misfit,
):
    tracers, levels, lat_rows, lon_cells = adjoint_in.shape
    slots = kernel_rows.shape[1]
    tiles = lax.axis_size("lon")
    parts = (levels + 15) // 16
    full = jax.ShapeDtypeStruct((tracers * levels * 8, 128), F32)
    planes = jax.ShapeDtypeStruct((levels * 8, 128), F32)
    rows_one = jax.ShapeDtypeStruct(((tracers + 3) * levels, 128), F32)
    columns_one = jax.ShapeDtypeStruct((tracers + 3, 8, 128), F32)
    rows_two = jax.ShapeDtypeStruct((2 * tracers * levels + 16, 128), F32)
    columns_two = jax.ShapeDtypeStruct((parts * 8, 128), F32)
    columns_sent = jax.ShapeDtypeStruct((parts * 8 + 16, 128), F32)

    packed = pl.pallas_call(
        pack_kernel,
        out_shape=jax.ShapeDtypeStruct((tiles, 80, 128), BF16),
        in_specs=[pl.BlockSpec(memory_space=pltpu.VMEM)] * 4,
        compiler_params=pltpu.CompilerParams(vmem_limit_bytes=56 << 20),
        name="pack",
    )(
        retrieval_counts.reshape(1, 1),
        kernel_rows,
        retrieval_misfit,
        retrieval_columns.reshape(slots // 128, 128),
    )
    packed, adjoint_in, wind_u, wind_v, diffusion = lax.optimization_barrier(
        (packed, adjoint_in, wind_u, wind_v, diffusion)
    )
    received = lax.all_to_all(packed, "lon", split_axis=0, concat_axis=0, tiled=True)

    field = adjoint_in.reshape(full.shape)
    u = wind_u.reshape(planes.shape)
    v = wind_v.reshape(planes.shape)
    k = diffusion.reshape(planes.shape)
    odd = jnp.stack([lax.axis_index("lat") & 1, lax.axis_index("lon") & 1])
    surface, *sent = vmem_call(
        prep_kernel,
        out_shape=(
            jax.ShapeDtypeStruct((tracers, 8, 128), F32),
            rows_one,
            rows_one,
            columns_one,
            columns_one,
        ),
        smem=3,
        name="prep",
    )(odd, station_cells, station_misfit, field, u, v, k)
    edges = swap(*sent[:2], "lat", False) + swap(*sent[2:], "lon", True)
    inverse = vmem_call(factor_kernel, out_shape=planes, name="factor")(k)
    ring = vmem_call(
        ring_kernel,
        out_shape=(planes,) * 4 + (columns_two,) * 2 + (planes,) * 2,
        smem=1,
        name="ring",
    )(odd, *edges)
    first = vmem_call(first_kernel, out_shape=full, smem=1, name="first")(
        odd, field, surface, u, v, k, inverse, *edges
    )
    edge, *sent = vmem_call(
        edge_kernel,
        out_shape=(
            jax.ShapeDtypeStruct((4, tracers * levels, 128), F32),
            rows_two,
            rows_two,
        ),
        smem=1,
        limit=30,
        name="edge",
    )(odd, received, first, u, v, inverse, *edges[:2])
    injected, east, west = vmem_call(
        inner_kernel, out_shape=(full, columns_two, columns_two), limit=30, name="inner"
    )(received, first, edge, u, v, inverse, *edges[:2])
    rows = swap(*sent, "lat", False)
    sent = vmem_call(relay_kernel, out_shape=(columns_sent,) * 2, smem=1, name="relay")(
        odd, *rows, east, west
    )
    columns = swap(*sent, "lon", True)
    last = vmem_call(
        last_kernel,
        out_shape=full,
        smem=1,
        scratch=(full,)
        + (planes,) * 4
        + (columns_two, planes, jax.ShapeDtypeStruct((2,) + columns_sent.shape, F32), full),
        copies=3 * tracers,
        name="last",
    )(odd, injected, u, v, k, inverse, *rows, *columns, west, east, *ring)
    return last.reshape(adjoint_in.shape)


def solution(mesh):
    return jax.shard_map(
        body,
        mesh=mesh,
        in_specs=(
            P(None, None, "lat", "lon"),
            P(None, "lat", "lon"),
            P(None, "lat", "lon"),
            P(None, "lat", "lon"),
            P(None, ("lat", "lon")),
            P(None, ("lat", "lon")),
            P(("lat", "lon")),
            P(("lat", "lon")),
            P(("lat", "lon")),
            P(None, ("lat", "lon")),
        ),
        out_specs=P(None, None, "lat", "lon"),
        check_vma=False,
    )
```
